128 devices in a mesh: group: 2 (over y_hi), win: 16 (over x, y_lo, core), mp: 4 (over z).
Axes of the slice: x: 4, y: 4 (y_hi: 2, y_lo: 2; y = y_hi * 2 + y_lo), z: 4, core: 2. Of those that a mesh axis runs over, the one named last changes fastest.
Arguments:
- tokens: bfloat16 [2, 4096, 4096], P('group', 'win', 'mp'), may hold values from -7 to 7, as said below
- proj: bfloat16 [2, 4096, 4096], P('group', None, 'mp'), may hold values from -1 to 1, as said below
- cotangent: bfloat16 [4096, 4096], P('win', 'mp'), may hold values from -6 to 6
- counts: int32 [16], P('win'), may hold values from 64 to 256, as said below
- frames: int32 [4096], P('win'), may hold values from 0 to 3, as said below
Outputs:
- input_grads: bfloat16 [2, 4096, 4096], P('group', 'win', 'mp')
- weight_grads: float32 [2, 4096, 4096], P('group', 'win', 'mp')
The draws below stay inside these ranges and needn't reach their ends.
Inputs may be any that keep to these rules, and one draw needn't show every extreme that they name: Every value lies within the range; proj slot 0 entries scale as 1 / sqrt(1024), slot 1 as 1 / sqrt(4096). `tokens`: finite values. `counts`: some window has all 256 slots live and some window exactly 64. Each window has a token that sees only the first frame and one that sees all frames.
All inputs are finite; a program needn't handle non-finite values.
Results may differ from the reference program's by a relative error of at most 0.015.
The reference program's roundings to bfloat16 on the way count: a program that leaves them out, or rounds other values in their place, can miss the bound.
Values may be sent and summed in bfloat16 or wider, within the bound.
A program may use at most 192 MiB of HBM per device.

```python
import jax
import jax.numpy as jnp
from jax import lax

D = 4096
DV = 1024
HEAD_DIM = 128
FRAMES = 4
NT = 256
ROWS = 4096
N_GROUP = 2
N_WIN = 16
N_MP = 4


def draw_tokens(key, part):
    first_key = jax.random.fold_in(key, 11)
    base_values = jnp.clip(jax.random.normal(first_key, (N_GROUP, ROWS, D), jnp.float32), -6.0, 6.0)
    return base_values.astype(jnp.bfloat16)


def draw_proj(key, part):
    first_key = jax.random.fold_in(key, 21)
    side_scale = jnp.array([DV ** (-0.5), D ** (-0.5)], jnp.float32)[:, None, None]
    base_values = jnp.clip(jax.random.normal(first_key, (N_GROUP, D, D), jnp.float32), -4.0, 4.0)
    return (base_values * side_scale).astype(jnp.bfloat16)


def draw_counts(key, part):
    first_key = jax.random.fold_in(key, 31)
    second_key = jax.random.fold_in(key, 32)
    drawn = jax.random.randint(first_key, (N_WIN,), NT // 4, NT + 1, jnp.int32)
    order = jax.random.permutation(second_key, N_WIN)
    drawn = drawn.at[order[0]].set(NT)
    drawn = drawn.at[order[1]].set(NT // 4)
    return drawn.astype(jnp.int32)


def draw_frames(key, part):
    first_key = jax.random.fold_in(key, 41)
    drawn = jax.random.randint(first_key, (N_WIN, NT), 0, FRAMES, jnp.int32)
    drawn = drawn.at[:, 0].set(FRAMES - 1)
    drawn = drawn.at[:, 1].set(0)
    return drawn.reshape(ROWS).astype(jnp.int32)


def block_levels(key, shape, split, smallest, high):
    gain = 1.0
    for axis_at, shards_of in split:
        draws = jax.random.uniform(jax.random.fold_in(jax.random.fold_in(key, 6), axis_at), (shards_of,), jnp.float32, smallest / len(split), high / len(split))
        gain = gain * jnp.repeat(jnp.exp(draws), shape[axis_at] // shards_of).reshape((-1,) + (1,) * (len(shape) - 1 - axis_at))
    return gain


def bell_draw(own_key, dims, spread, bound, pieces=(), kind=jnp.bfloat16):
    result = spread * jax.random.normal(own_key, dims, jnp.float32)
    if pieces:
        result = result * block_levels(own_key, dims, pieces, -0.22, 0.18)
    return jnp.clip(result, -bound, bound).astype(kind)


def setup_inputs(seed: int = 0) -> dict:
    seeds = jax.random.split(jax.random.key(seed), 6)
    tokens = draw_tokens(jax.random.fold_in(seeds[5], 71), 0)
    proj = draw_proj(jax.random.fold_in(seeds[5], 71), 0)
    cotangent = bell_draw(seeds[2], (ROWS, D), 1.0, 6.0, ((0, 16), (1, 4)))
    counts = draw_counts(jax.random.fold_in(seeds[5], 71), 0)
    frames = draw_frames(jax.random.fold_in(seeds[5], 71), 0)
    return dict(tokens=tokens, proj=proj, cotangent=cotangent, counts=counts, frames=frames)


def soft_grads(queries, key_rows, value_rows, upstream, allowed, factor):
    scores = jnp.einsum("qhd,khd->hqk", queries, key_rows) * factor
    scores = jnp.where(allowed[None], scores, -1e30)
    top_score = jnp.max(scores, axis=-1, keepdims=True)
    shifted = jnp.exp(scores - top_score)
    attention = shifted / jnp.sum(shifted, axis=-1, keepdims=True)
    rounded = lax.optimization_barrier(attention.astype(jnp.bfloat16)).astype(jnp.float32)
    value_grad = jnp.einsum("hqk,qhd->khd", rounded, upstream).astype(jnp.bfloat16)
    attn_grad = jnp.einsum("qhd,khd->hqk", upstream, value_rows)
    score_grad = attention * (attn_grad - jnp.sum(attention * attn_grad, axis=-1, keepdims=True)) * factor
    score_grad = lax.optimization_barrier(score_grad.astype(jnp.bfloat16)).astype(jnp.float32)
    query_grad = jnp.einsum("hqk,khd->qhd", score_grad, key_rows).astype(jnp.bfloat16)
    key_grad = jnp.einsum("hqk,qhd->khd", score_grad, queries).astype(jnp.bfloat16)
    return query_grad, key_grad, value_grad


def reference(tokens, proj, cotangent, counts, frames):
    video_rows = NT * (D // DV)
    head_count = D // HEAD_DIM
    factor = HEAD_DIM ** -0.5
    w_key = proj[0, :DV, :]
    w_value = proj[0, DV:2 * DV, :]
    w_query = proj[1]
    key_frame = jnp.arange(video_rows, dtype=jnp.int32) // (video_rows // FRAMES)
    block_width = D // N_MP

    def heads_of(array):
        return array.astype(jnp.float32).reshape(array.shape[0], head_count, HEAD_DIM)

    def window(carry, window_index):
        grad_query, grad_key, grad_value = carry
        begin = (window_index * NT).astype(jnp.int32)
        features = lax.dynamic_slice_in_dim(tokens[0], begin, NT, 0).reshape(video_rows, DV)
        neurons = lax.dynamic_slice_in_dim(tokens[1], begin, NT, 0)
        cot_rows = lax.dynamic_slice_in_dim(cotangent, begin, NT, 0)
        frame_rows = lax.dynamic_slice_in_dim(frames, begin, NT, 0)
        live_rows = jnp.arange(NT, dtype=jnp.int32) < counts[window_index]
        key_rows = jnp.dot(features, w_key, preferred_element_type=jnp.float32).astype(jnp.bfloat16)
        value_rows = jnp.dot(features, w_value, preferred_element_type=jnp.float32).astype(jnp.bfloat16)
        queries = jnp.dot(neurons, w_query, preferred_element_type=jnp.float32).astype(jnp.bfloat16)
        upstream = jnp.where(live_rows[:, None], cot_rows, jnp.zeros_like(cot_rows))
        allowed = key_frame[None, :] <= frame_rows[:, None]
        query_grad, key_grad, value_grad = soft_grads(heads_of(queries), heads_of(key_rows), heads_of(value_rows), heads_of(upstream), allowed, factor)
        query_grad = query_grad.reshape(NT, D)
        key_grad = key_grad.reshape(video_rows, D)
        value_grad = value_grad.reshape(video_rows, D)
        grad_query = grad_query + jnp.dot(neurons.T, query_grad, preferred_element_type=jnp.float32)
        grad_key = grad_key + jnp.dot(features.T, key_grad, preferred_element_type=jnp.float32)
        grad_value = grad_value + jnp.dot(features.T, value_grad, preferred_element_type=jnp.float32)
        neuron_sum = jnp.zeros((NT, D), jnp.float32)
        feature_sum = jnp.zeros((video_rows, DV), jnp.float32)
        for shard_index in range(N_MP):
            first_col = shard_index * block_width
            last_col = first_col + block_width
            neuron_part = jnp.dot(query_grad[:, first_col:last_col], w_query[:, first_col:last_col].T, preferred_element_type=jnp.float32)
            neuron_sum = neuron_sum + lax.optimization_barrier(neuron_part.astype(jnp.bfloat16)).astype(jnp.float32)
            feature_part = jnp.dot(key_grad[:, first_col:last_col], w_key[:, first_col:last_col].T, preferred_element_type=jnp.float32)
            feature_part = feature_part + jnp.dot(value_grad[:, first_col:last_col], w_value[:, first_col:last_col].T, preferred_element_type=jnp.float32)
            feature_sum = feature_sum + lax.optimization_barrier(feature_part.astype(jnp.bfloat16)).astype(jnp.float32)
        neuron_out = (cot_rows.astype(jnp.float32) + neuron_sum).astype(jnp.bfloat16)
        feature_out = feature_sum.astype(jnp.bfloat16).reshape(NT, D)
        return (grad_query, grad_key, grad_value), (feature_out, neuron_out)

    start_carry = (jnp.zeros((D, D), jnp.float32), jnp.zeros((DV, D), jnp.float32), jnp.zeros((DV, D), jnp.float32))
    sums, outs = lax.scan(window, start_carry, jnp.arange(N_WIN, dtype=jnp.int32))
    grad_query, grad_key, grad_value = sums
    feature_outs, neuron_outs = outs
    input_grads = jnp.stack([feature_outs.reshape(N_WIN * NT, D), neuron_outs.reshape(N_WIN * NT, D)])
    video_slot = jnp.concatenate([grad_key, grad_value, jnp.zeros((D - 2 * DV, D), jnp.float32)], 0)
    weight_grads = jnp.stack([video_slot, grad_query])
    return input_grads, weight_grads
```

```python
import jax
import jax.numpy as jnp
from jax import lax
from jax.experimental import pallas as pl
from jax.experimental.pallas import tpu as pltpu
from jax.sharding import PartitionSpec as P

MESH = pl.DeviceIdType.MESH
BF = jnp.bfloat16
F32 = jnp.float32
FACTOR = 128 ** (-0.5)
BLK = 256
WIDE = 1024
HALF = 128


def nn(a, b):
    return jnp.dot(a, b, preferred_element_type=F32)


def nt(a, b):
    return lax.dot_general(a, b, (((1,), (1,)), ((), ())), preferred_element_type=F32)


def tn(a, b):
    return lax.dot_general(a, b, (((0,), (0,)), ((), ())), preferred_element_type=F32)


def ds(i, size):
    return pl.ds(pl.multiple_of(i * size, size), size)


def rcopy(src, dst, send_sem, recv_sem, device):
    return pltpu.make_async_remote_copy(
        src_ref=src,
        dst_ref=dst,
        send_sem=send_sem,
        recv_sem=recv_sem,
        device_id=device,
        device_id_type=MESH,
    )


def kernel(
    tok, proj, cot, counts, frames, ig, wg,
    TOK, W, COT, ACC, Q, U, BIAS, K, V, S, DP, KG, VG, QG, FT, TOKX, QGX,
    CS, CR, KEEP, X1S, X1R, X2S, X2R, YS, YR, PS, RAL, RAR, RBL, RBR,
    l_sem, ag_s, ag_r, q_s, q_r, qg_s, qg_r, aa_s, aa_r, xg_s, xg_r,
    cs_s, cs_r, x1_s, x1_r, x2_s, x2_r, y_s, y_r, rs_s, rs_r,
):
    g = lax.axis_index("group")
    w = lax.axis_index("win")
    m = lax.axis_index("mp")
    x = w // 4
    yl = (w // 2) % 2
    c = w % 2
    is_video = g == 0
    is_neural = g == 1
    right_m, left_m, far_m = (m + 1) % 4, (m + 3) % 4, (m + 2) % 4
    right, left = {"mp": right_m}, {"mp": left_m}
    partner = {"group": 1 - g}
    core = {"win": w + 1 - 2 * c}
    yside = {"win": w + 2 - 4 * yl}

    def xdev(xp):
        return {"win": xp * 4 + w % 4}

    xnear = xdev(x + 1 - 2 * (x % 2))
    xback = xdev(3 - x)
    keep_kind = ((x + 1) // 2) % 2

    load_tok = pltpu.make_async_copy(tok.at[0], TOK.at[m], l_sem.at[0])
    load_tok.start()
    load_cot = pltpu.make_async_copy(cot, COT, l_sem.at[1])

    def load_w(i, b):
        return pltpu.make_async_copy(proj.at[0, ds(b, WIDE)], W.at[b], l_sem.at[2 + i])

    order = (m, left_m, right_m, far_m)

    @pl.when(is_neural)
    def _():
        for i in range(4):
            load_w(i, order[i]).start()

    @pl.when(is_video)
    def _():
        for i in range(2):
            load_w(i, i).start()

    load_cot.start()

    barrier = pltpu.get_barrier_semaphore()
    greet = [right, left, partner, core, yside] + [xdev((x + d) % 4) for d in (1, 2, 3)]
    for device in greet:
        pl.semaphore_signal(barrier, inc=1, device_id=device, device_id_type=MESH)
    pl.semaphore_wait(barrier, len(greet))

    lo, hi = pl.ds(0, HALF), pl.ds(HALF, HALF)

    def ring(i, block, rows, device):
        return rcopy(TOK.at[block, rows], TOK.at[block, rows], ag_s.at[i], ag_r.at[i], device)

    load_tok.wait()
    ring(0, m, lo, right).start()
    ring(2, m, hi, left).start()
    ring(1, m, hi, right).start()
    ring(3, m, lo, left).start()

    def project(b, i):
        @pl.when(is_video)
        def _():
            if i == 0:
                load_w(0, 0).wait()
                load_w(1, 1).wait()
            rows = ds(b, BLK)
            for j in range(4):
                cols = pl.ds(j * BLK, BLK)
                K[rows, cols] = nn(TOK[b], W[0, :, cols]).astype(BF)
                V[rows, cols] = nn(TOK[b], W[1, :, cols]).astype(BF)
            FT[:, rows] = TOK[b].T

        @pl.when(is_neural)
        def _():
            load_w(i, b).wait()
            for j in range(4):
                cols = pl.ds(j * BLK, BLK)
                part = nn(TOK[b], W[b, :, cols])
                if i == 0:
                    ACC[:, cols] = part
                elif i < 3:
                    ACC[:, cols] += part
                else:
                    Q[j] = (ACC[:, cols] + part).astype(BF)
                    rcopy(Q.at[j], Q.at[j], q_s.at[j], q_r.at[j], partner).start()

    project(m, 0)
    ring(0, left_m, lo, left).wait_recv()
    ring(4, left_m, lo, right).start()
    ring(2, right_m, hi, right).wait_recv()
    ring(5, right_m, hi, left).start()
    ring(1, left_m, hi, left).wait_recv()
    project(left_m, 1)
    ring(3, right_m, lo, right).wait_recv()
    project(right_m, 2)

    @pl.when(is_video)
    def _():
        load_cot.wait()
        live = lax.broadcasted_iota(jnp.int32, (BLK, BLK), 0) < counts[0]
        for j in range(4):
            part = COT[:, pl.ds(j * BLK, BLK)].astype(F32)
            U[j] = jnp.where(live, part, jnp.zeros_like(part)).astype(BF)
        key_frame = lax.broadcasted_iota(jnp.int32, (BLK, BLK), 0) >> 6
        BIAS[...] = jnp.where(key_frame <= frames[...], 0.0, -1e30).astype(F32)

    ring(4, far_m, lo, left).wait_recv()
    ring(5, far_m, hi, right).wait_recv()
    project(far_m, 3)

    def core_send(p, count):
        return rcopy(CS.at[p, pl.ds(0, count)], CR.at[p, pl.ds(0, count)], cs_s.at[p], cs_r.at[p], core)

    def weight_part(p, kinds, rhs):
        for kind in range(kinds):
            for yd in range(2):
                CS[p, kind * 2 + yd] = nn(FT[ds(2 * yd + 1 - c, BLK)], rhs(kind)).astype(BF)
        core_send(p, 2 * kinds).start()
        for kind in range(kinds):
            for yd in range(2):
                KEEP[p, kind * 2 + yd] = nn(FT[ds(2 * yd + c, BLK)], rhs(kind))

    def y_send(p):
        return rcopy(YS.at[p], YR.at[p], y_s.at[p], y_r.at[p], yside)

    def x1_send(p):
        return rcopy(X1S.at[p], X1R.at[p], x1_s.at[p], x1_r.at[p], xnear)

    def x2_send(p):
        return rcopy(X2S.at[p], X2R.at[p], x2_s.at[p], x2_r.at[p], xback)

    def part_send(i):
        src = (
            PS.at[far_m, lo], PS.at[right_m, hi], PS.at[right_m, lo],
            PS.at[far_m, hi], PS.at[left_m, lo], PS.at[left_m, hi],
        )[i]
        dst = (RAL, RBL.at[hi], RBL.at[lo], RAR, RBR.at[lo], RBR.at[hi])[i]
        return rcopy(src, dst, rs_s.at[i], rs_r.at[i], right if i < 3 else left)

    def input_parts(part):
        part(far_m)
        part_send(0).start()
        part_send(3).start()
        part(right_m)
        part_send(1).start()
        part(left_m)
        part_send(4).start()
        part(m)

    def input_forward():
        part_send(0).wait_recv()
        PS[right_m, lo] = (PS[right_m, lo].astype(F32) + RAL[...].astype(F32)).astype(BF)
        part_send(2).start()
        part_send(3).wait_recv()
        PS[left_m, hi] = (PS[left_m, hi].astype(F32) + RAR[...].astype(F32)).astype(BF)
        part_send(5).start()

    def input_total():
        for i in (1, 2, 4, 5):
            part_send(i).wait_recv()
        return PS[m].astype(F32) + RBL[...].astype(F32) + RBR[...].astype(F32)

    def qg_send(p):
        return rcopy(QG.at[p], QGX.at[p, ds(x, BLK)], qg_s.at[p], qg_r.at[p], partner)

    @pl.when(is_video)
    def _():
        def attend(p, hh):
            cols = ds(2 * p + hh, HALF)
            head = pl.ds(hh * HALF, HALF)
            q = Q[p, :, head]
            u = U[p, :, head]
            top = None
            for t in range(4):
                s = nt(K[pl.ds(t * BLK, BLK), cols], q) + BIAS[...]
                S[t] = s
                high = jnp.max(s, axis=0, keepdims=True)
                top = high if top is None else jnp.maximum(top, high)
            total = jnp.zeros_like(top)
            weighted = jnp.zeros_like(top)
            for t in range(4):
                e = jnp.exp((S[t] - top) * FACTOR)
                d = nt(V[pl.ds(t * BLK, BLK), cols], u)
                S[t] = e
                DP[t] = d
                total += jnp.sum(e, axis=0, keepdims=True)
                weighted += jnp.sum(e * d, axis=0, keepdims=True)
            inverse = 1.0 / total
            mean = weighted * inverse
            query_grad = None
            for t in range(4):
                a = S[t] * inverse
                VG[pl.ds(t * BLK, BLK), cols] = nn(a.astype(BF), u).astype(BF)
                sg = (a * (DP[t] - mean) * FACTOR).astype(BF)
                KG[pl.ds(t * BLK, BLK), cols] = nn(sg, q).astype(BF)
                more = tn(sg, K[pl.ds(t * BLK, BLK), cols])
                query_grad = more if query_grad is None else query_grad + more
            QG[p, :, head] = query_grad.astype(BF)

        def stage_x1(p):
            core_send(p, 4).wait_recv()
            for yd in range(2):
                i = (1 - keep_kind) * 2 + yd
                X1S[p, yd] = (KEEP[p, i] + CR[p, i].astype(F32)).astype(BF)
            x1_send(p).start()
            for yd in range(2):
                i = keep_kind * 2 + yd
                KEEP[p, i] = KEEP[p, i] + CR[p, i].astype(F32)

        def stage_x2(p):
            x1_send(p).wait_recv()
            for yd in range(2):
                i = keep_kind * 2 + yd
                total = KEEP[p, i] + X1R[p, yd].astype(F32)
                KEEP[p, i] = total
                X2S[p, yd] = total.astype(BF)

            @pl.when(x >= 2)
            def _():
                x2_send(p).start()

        def stage_y(p):
            @pl.when(x < 2)
            def _():
                x2_send(p).wait_recv()
                i = keep_kind * 2 + 1 - yl
                YS[p] = (KEEP[p, i] + X2R[p, 1 - yl].astype(F32)).astype(BF)
                y_send(p).start()
                i = keep_kind * 2 + yl
                KEEP[p, i] = KEEP[p, i] + X2R[p, yl].astype(F32)

        def step(p, carry):
            rcopy(Q.at[p], Q.at[p], q_s.at[p], q_r.at[p], partner).wait_recv()
            for hh in range(2):
                attend(p, hh)
            qg_send(p).start()
            cols = ds(p, BLK)
            weight_part(p, 2, lambda kind: (KG, VG)[kind][:, cols])

            @pl.when(p >= 1)
            def _():
                stage_x1(p - 1)

            @pl.when(p >= 2)
            def _():
                stage_x2(p - 2)

            @pl.when(p >= 3)
            def _():
                stage_y(p - 3)

            return carry

        lax.fori_loop(0, 4, step, 0)

        def part(d):
            rows = ds(d, BLK)
            for j in range(4):
                out = pl.ds(j * BLK, BLK)
                PS[d, :, out] = (nt(KG[rows], W[0, out]) + nt(VG[rows], W[1, out])).astype(BF)

        input_parts(part)
        stage_x1(3)
        stage_x2(2)
        input_forward()
        stage_y(1)
        stage_x2(3)
        stage_y(2)
        stage_y(3)
        ig[0] = input_total().astype(BF)

        @pl.when(x < 2)
        def _():
            for p in range(4):
                y_send(p).wait_recv()
                wg[0, :, pl.ds(p * BLK, BLK)] = KEEP[p, keep_kind * 2 + yl] + YR[p].astype(F32)

        @pl.when(x >= 2)
        def _():
            wg[...] = jnp.zeros_like(wg)

        for p in range(4):
            qg_send(p).wait_send()
            core_send(p, 4).wait_send()
            x1_send(p).wait_send()

        @pl.when(x >= 2)
        def _():
            for p in range(4):
                x2_send(p).wait_send()

        @pl.when(x < 2)
        def _():
            for p in range(4):
                y_send(p).wait_send()

    @pl.when(is_neural)
    def _():
        def swap_send(d):
            return rcopy(TOK.at[(x + d) % 4], TOKX.at[x], aa_s.at[d - 1], aa_r.at[d - 1], xdev((x + d) % 4))

        def swap_recv(d):
            s = TOKX.at[(x + 4 - d) % 4]
            return rcopy(s, s, aa_s.at[d - 1], aa_r.at[d - 1], xdev((x + d) % 4))

        for d in (1, 3, 2):
            swap_send(d).start()
        FT[:, ds(x, BLK)] = TOK[x].T
        for d in (1, 3, 2):
            swap_recv(d).wait_recv()
            FT[:, ds((x + 4 - d) % 4, BLK)] = TOKX[(x + 4 - d) % 4].T

        def gather_send(p, d):
            s = QGX.at[p, ds(x, BLK)]
            return rcopy(s, s, xg_s.at[p, d - 1], xg_r.at[p, d - 1], xdev((x + d) % 4))

        def gather_recv(p, d):
            s = QGX.at[p, ds((x + 4 - d) % 4, BLK)]
            return rcopy(s, s, xg_s.at[p, d - 1], xg_r.at[p, d - 1], xdev((x + d) % 4))

        def relay(p):
            qg_send(p).wait_recv()
            for d in (1, 3, 2):
                gather_send(p, d).start()

        def chunk(p):
            for d in (1, 3, 2):
                gather_recv(p, d).wait_recv()
            weight_part(p, 1, lambda kind: QGX[p])

        def stage_y(p):
            core_send(p, 2).wait_recv()
            YS[p] = (KEEP[p, 1 - yl] + CR[p, 1 - yl].astype(F32)).astype(BF)
            y_send(p).start()
            KEEP[p, yl] = KEEP[p, yl] + CR[p, yl].astype(F32)

        def part(d):
            for j in range(4):
                out = pl.ds(j * BLK, BLK)
                total = None
                for p in range(4):
                    more = nt(QGX[p, ds(x, BLK)], W[d, out, pl.ds(p * BLK, BLK)])
                    total = more if total is None else total + more
                PS[d, :, out] = total.astype(BF)

        for p in range(4):
            relay(p)
        input_parts(part)
        chunk(0)
        input_forward()
        stage_y(0)
        for p in range(1, 4):
            chunk(p)
            stage_y(p)
        load_cot.wait()
        ig[0] = (input_total() + COT[...].astype(F32)).astype(BF)
        for p in range(4):
            y_send(p).wait_recv()
            wg[0, :, pl.ds(p * BLK, BLK)] = KEEP[p, yl] + YR[p].astype(F32)
        for p in range(4):
            rcopy(Q.at[p], Q.at[p], q_s.at[p], q_r.at[p], partner).wait_send()
            core_send(p, 2).wait_send()
            y_send(p).wait_send()
            for d in (1, 3, 2):
                gather_send(p, d).wait_send()
        for d in (1, 3, 2):
            swap_send(d).wait_send()

    ring(0, m, lo, right).wait_send()
    ring(2, m, hi, left).wait_send()
    ring(1, m, hi, right).wait_send()
    ring(3, m, lo, left).wait_send()
    ring(4, left_m, lo, right).wait_send()
    ring(5, right_m, hi, left).wait_send()
    for i in range(6):
        part_send(i).wait_send()


def local(tokens, proj, cotangent, counts, frames):
    vmem = pltpu.VMEM
    dma = pltpu.SemaphoreType.DMA
    scratch = [
        vmem((4, BLK, WIDE), BF),
        vmem((4, WIDE, WIDE), BF),
        vmem((BLK, WIDE), BF),
        vmem((BLK, WIDE), F32),
        vmem((4, BLK, BLK), BF),
        vmem((4, BLK, BLK), BF),
        vmem((BLK, BLK), F32),
        vmem((WIDE, WIDE), BF),
        vmem((WIDE, WIDE), BF),
        vmem((4, BLK, BLK), F32),
        vmem((4, BLK, BLK), F32),
        vmem((WIDE, WIDE), BF),
        vmem((WIDE, WIDE), BF),
        vmem((4, BLK, BLK), BF),
        vmem((WIDE, WIDE), BF),
        vmem((4, BLK, WIDE), BF),
        vmem((4, WIDE, BLK), BF),
        vmem((4, 4, BLK, BLK), BF),
        vmem((4, 4, BLK, BLK), BF),
        vmem((4, 4, BLK, BLK), F32),
        vmem((4, 2, BLK, BLK), BF),
        vmem((4, 2, BLK, BLK), BF),
        vmem((4, 2, BLK, BLK), BF),
        vmem((4, 2, BLK, BLK), BF),
        vmem((4, BLK, BLK), BF),
        vmem((4, BLK, BLK), BF),
        vmem((4, BLK, WIDE), BF),
        vmem((HALF, WIDE), BF),
        vmem((HALF, WIDE), BF),
        vmem((BLK, WIDE), BF),
        vmem((BLK, WIDE), BF),
        dma((6,)),
        dma((6,)), dma((6,)),
        dma((4,)), dma((4,)),
        dma((4,)), dma((4,)),
        dma((3,)), dma((3,)),
        dma((4, 3)), dma((4, 3)),
        dma((4,)), dma((4,)),
        dma((4,)), dma((4,)),
        dma((4,)), dma((4,)),
        dma((4,)), dma((4,)),
        dma((6,)), dma((6,)),
    ]
    anywhere = pl.BlockSpec(memory_space=pl.ANY)
    in_vmem = pl.BlockSpec(memory_space=vmem)
    return pl.pallas_call(
        kernel,
        out_shape=(
            jax.ShapeDtypeStruct((1, BLK, WIDE), BF),
            jax.ShapeDtypeStruct((1, BLK, WIDE), F32),
        ),
        in_specs=[
            anywhere, anywhere, anywhere,
            pl.BlockSpec(memory_space=pltpu.SMEM),
            in_vmem,
        ],
        out_specs=(in_vmem, in_vmem),
        scratch_shapes=scratch,
        compiler_params=pltpu.CompilerParams(
            collective_id=0, has_side_effects=True, vmem_limit_bytes=60 * 2**20
        ),
        cost_estimate=pl.CostEstimate(
            flops=20 * 10**9, bytes_accessed=16 * 2**20, transcendentals=2**21
        ),
    )(tokens, proj, cotangent, counts, frames.reshape(1, BLK))


def solution(mesh):
    return jax.shard_map(
        local,
        mesh=mesh,
        in_specs=(
            P("group", "win", "mp"),
            P("group", None, "mp"),
            P("win", "mp"),
            P("win"),
            P("win"),
        ),
        out_specs=(P("group", "win", "mp"), P("group", "win", "mp")),
        check_vma=False,
    )
```

```python
import jax
import jax.numpy as jnp
from jax import lax
from jax.experimental import pallas as pl
from jax.experimental.pallas import tpu as pltpu
from jax.sharding import PartitionSpec as P

MESH = pl.DeviceIdType.MESH
BF = jnp.bfloat16
F32 = jnp.float32
FACTOR = 128 ** (-0.5)
LOG2_E = 1.4426950408889634
BLK = 256
WIDE = 1024
HALF = 128
PIECE = 64


def nn(a, b):
    return jnp.dot(a, b, preferred_element_type=F32)


def nt(a, b):
    return lax.dot_general(a, b, (((1,), (1,)), ((), ())), preferred_element_type=F32)


def tn(a, b):
    return lax.dot_general(a, b, (((0,), (0,)), ((), ())), preferred_element_type=F32)


def ds(i, size):
    return pl.ds(pl.multiple_of(i * size, size), size)


def rcopy(src, dst, send_sem, recv_sem, device):
    return pltpu.make_async_remote_copy(
        src_ref=src,
        dst_ref=dst,
        send_sem=send_sem,
        recv_sem=recv_sem,
        device_id=device,
        device_id_type=MESH,
    )


def kernel(
    tok, proj, cot, counts, frames, ig, wg,
    TOK, W, COT, ACC, Q, U, BIAS, K, KT, V, S, DP, KG, VG, QG, FT, TOKX, QGX,
    CS, CR, KEEP, X1S, X1R, X2S, X2R, YS, YR, ZS, ZR, PS, RAL, RAR, RBL, RBR,
    l_sem, ag_s, ag_r, q_s, q_r, qg_s, qg_r, aa_s, aa_r, ar_s, ar_r, xg_s, xg_r,
    cs_s, cs_r, x1_s, x1_r, x2_s, x2_r, y_s, y_r, z_s, z_r, rs_s, rs_r,
):
    g = lax.axis_index("group")
    w = lax.axis_index("win")
    m = lax.axis_index("mp")
    x = w // 4
    yl = (w // 2) % 2
    c = w % 2
    is_video = g == 0
    is_neural = g == 1
    right_m, left_m, far_m = (m + 1) % 4, (m + 3) % 4, (m + 2) % 4
    right, left = {"mp": right_m}, {"mp": left_m}
    partner = {"group": 1 - g}
    core = {"win": w + 1 - 2 * c}
    yside = {"win": w + 2 - 4 * yl}

    def xdev(xp):
        return {"win": xp * 4 + w % 4}

    xnear = xdev(x + 1 - 2 * (x % 2))
    xback = xdev(3 - x)
    keep_kind = ((x + 1) // 2) % 2

    load_tok = pltpu.make_async_copy(tok.at[0], TOK.at[m], l_sem.at[0])
    load_tok.start()
    load_cot = pltpu.make_async_copy(cot, COT, l_sem.at[1])

    def load_w(i, b):
        return pltpu.make_async_copy(proj.at[0, ds(b, WIDE)], W.at[b], l_sem.at[2 + i])

    order = (m, left_m, right_m, far_m)

    @pl.when(is_neural)
    def _():
        for i in range(4):
            load_w(i, order[i]).start()

    @pl.when(is_video)
    def _():
        for i in range(2):
            load_w(i, i).start()

    load_cot.start()

    barrier = pltpu.get_barrier_semaphore()
    greet = [right, left, partner, core, yside] + [xdev((x + d) % 4) for d in (1, 2, 3)]
    for device in greet:
        pl.semaphore_signal(barrier, inc=1, device_id=device, device_id_type=MESH)
    pl.semaphore_wait(barrier, len(greet))

    lo, hi = pl.ds(0, HALF), pl.ds(HALF, HALF)

    def ring(half, i, block):
        device = right if i in (0, 1, 4) else left
        start = half * HALF + (0 if i in (0, 3, 4) else PIECE)
        rows = pl.ds(start, PIECE)
        return rcopy(TOK.at[block, rows], TOK.at[block, rows], ag_s.at[half, i], ag_r.at[half, i], device)

    def ring_start(half):
        for i in (0, 2, 1, 3):
            ring(half, i, m).start()

    def ring_forward(half):
        ring(half, 0, left_m).wait_recv()
        ring(half, 4, left_m).start()
        ring(half, 2, right_m).wait_recv()
        ring(half, 5, right_m).start()

    def q_send(j, half):
        s = Q.at[j, pl.ds(half * HALF, HALF)]
        return rcopy(s, s, q_s.at[j, half], q_r.at[j, half], partner)

    def project(b, i, half):
        rows = pl.ds(half * HALF, HALF)

        @pl.when(is_video)
        def _():
            if i == 0 and half == 0:
                load_w(0, 0).wait()
                load_w(1, 1).wait()
            keys = ds(2 * b + half, HALF)
            for j in range(4):
                cols = pl.ds(j * BLK, BLK)
                K[keys, cols] = nn(TOK[b, rows], W[0, :, cols]).astype(BF)
                V[keys, cols] = nn(TOK[b, rows], W[1, :, cols]).astype(BF)
            FT[:, keys] = TOK[b, rows].T
            KT[:, keys] = K[keys].T

        @pl.when(is_neural)
        def _():
            if half == 0:
                load_w(i, b).wait()
            for j in range(4):
                cols = pl.ds(j * BLK, BLK)
                part = nn(TOK[b, rows], W[b, :, cols])
                if i == 0:
                    ACC[rows, cols] = part
                elif i < 3:
                    ACC[rows, cols] += part
                else:
                    Q[j, rows] = (ACC[rows, cols] + part).astype(BF)
                    q_send(j, half).start()

    eighth = HALF // 4

    def swap_send(half, d):
        rows = ds(4 * half + m, eighth)
        return rcopy(
            TOK.at[(x + d) % 4, rows], TOKX.at[x, rows],
            aa_s.at[half, d - 1], aa_r.at[half, d - 1], xdev((x + d) % 4),
        )

    def swap_recv(half, d):
        s = TOKX.at[(x + 4 - d) % 4, ds(4 * half + m, eighth)]
        return rcopy(s, s, aa_s.at[half, d - 1], aa_r.at[half, d - 1], xdev((x + d) % 4))

    load_tok.wait()
    ring_start(0)
    project(m, 0, 0)
    ring_forward(0)
    ring_start(1)
    ring(0, 1, left_m).wait_recv()
    project(left_m, 1, 0)
    ring(0, 3, right_m).wait_recv()
    project(right_m, 2, 0)
    ring(0, 4, far_m).wait_recv()
    ring(0, 5, far_m).wait_recv()
    project(far_m, 3, 0)

    @pl.when(is_neural)
    def _():
        for d in (1, 3, 2):
            swap_send(0, d).start()

    project(m, 0, 1)
    ring_forward(1)
    ring(1, 1, left_m).wait_recv()
    project(left_m, 1, 1)
    ring(1, 3, right_m).wait_recv()
    project(right_m, 2, 1)

    @pl.when(is_video)
    def _():
        load_cot.wait()
        live = lax.broadcasted_iota(jnp.int32, (BLK, BLK), 0) < counts[0]
        for j in range(4):
            part = COT[:, pl.ds(j * BLK, BLK)].astype(F32)
            U[j] = jnp.where(live, part, jnp.zeros_like(part)).astype(BF)
        key_frame = lax.broadcasted_iota(jnp.int32, (BLK, BLK), 0) >> 6
        BIAS[...] = jnp.where(key_frame <= frames[...], 0.0, -1e30).astype(F32)

    ring(1, 4, far_m).wait_recv()
    ring(1, 5, far_m).wait_recv()
    project(far_m, 3, 1)

    def core_send(p, count):
        return rcopy(CS.at[p, pl.ds(0, count)], CR.at[p, pl.ds(0, count)], cs_s.at[p], cs_r.at[p], core)

    def weight_part(p, kinds, rhs):
        for kind in range(kinds):
            for yd in range(2):
                CS[p, kind * 2 + yd] = nn(FT[ds(2 * yd + 1 - c, BLK)], rhs(kind)).astype(BF)
        core_send(p, 2 * kinds).start()
        for kind in range(kinds):
            for yd in range(2):
                KEEP[p, kind * 2 + yd] = nn(FT[ds(2 * yd + c, BLK)], rhs(kind))

    def y_send(p):
        return rcopy(YS.at[p], YR.at[p], y_s.at[p], y_r.at[p], yside)

    def x1_send(p, n):
        some = pl.ds(0, n)
        return rcopy(X1S.at[p, some], X1R.at[p, some], x1_s.at[p], x1_r.at[p], xnear)

    def x2_send(p, n):
        some = pl.ds(0, n)
        return rcopy(X2S.at[p, some], X2R.at[p, some], x2_s.at[p], x2_r.at[p], xback)

    def part_send(i):
        src = (
            PS.at[far_m, lo], PS.at[right_m, hi], PS.at[right_m, lo],
            PS.at[far_m, hi], PS.at[left_m, lo], PS.at[left_m, hi],
        )[i]
        dst = (RAL, RBL.at[hi], RBL.at[lo], RAR, RBR.at[lo], RBR.at[hi])[i]
        return rcopy(src, dst, rs_s.at[i], rs_r.at[i], right if i < 3 else left)

    def input_parts(part, first, second, third):
        part(far_m)
        part_send(0).start()
        part_send(3).start()
        first()
        part(right_m)
        part_send(1).start()
        part(left_m)
        part_send(4).start()
        second()
        part(m)
        third()

    def input_forward():
        part_send(0).wait_recv()
        PS[right_m, lo] = (PS[right_m, lo].astype(F32) + RAL[...].astype(F32)).astype(BF)
        part_send(2).start()
        part_send(3).wait_recv()
        PS[left_m, hi] = (PS[left_m, hi].astype(F32) + RAR[...].astype(F32)).astype(BF)
        part_send(5).start()

    def input_total():
        for i in (1, 2, 4, 5):
            part_send(i).wait_recv()
        return PS[m].astype(F32) + RBL[...].astype(F32) + RBR[...].astype(F32)

    def qg_send(p):
        return rcopy(QG.at[p], QGX.at[p, ds(x, BLK)], qg_s.at[p], qg_r.at[p], partner)

    @pl.when(is_video)
    def _():
        def attend(p):
            blocks = [pl.ds(t * BLK, BLK) for t in range(4)]

            def scores(hh):
                cols = ds(2 * p + hh, HALF)
                head = pl.ds(hh * HALF, HALF)
                q = Q[p, :, head]
                u = U[p, :, head]
                q_t = q.T
                top = None
                for t in range(4):
                    s = nn(K[blocks[t], cols], q_t) + BIAS[...]
                    S[4 * hh + t] = s
                    high = jnp.max(s, axis=0, keepdims=True)
                    top = high if top is None else jnp.maximum(top, high)
                return cols, head, q, u, top

            def weights(hh, cols, u, top):
                u_t = u.T
                total = jnp.zeros_like(top)
                weighted = jnp.zeros_like(top)
                for t in range(4):
                    e = jnp.exp2((S[4 * hh + t] - top) * (FACTOR * LOG2_E))
                    d = nn(V[blocks[t], cols], u_t)
                    S[4 * hh + t] = e
                    DP[4 * hh + t] = d
                    total += jnp.sum(e, axis=0, keepdims=True)
                    weighted += jnp.sum(e * d, axis=0, keepdims=True)
                inverse = 1.0 / total
                return inverse, weighted * inverse

            def grads(hh, cols, head, q, u, inverse, mean):
                query_grad = None
                for t in range(4):
                    a = S[4 * hh + t] * inverse
                    VG[blocks[t], cols] = nn(a.astype(BF), u).astype(BF)
                    sg = (a * (DP[4 * hh + t] - mean) * FACTOR).astype(BF)
                    KG[blocks[t], cols] = nn(sg, q).astype(BF)
                    more = nn(KT[cols, blocks[t]], sg)
                    query_grad = more if query_grad is None else query_grad + more
                QG[p, :, head] = query_grad.T.astype(BF)

            cols0, head0, q0, u0, top0 = scores(0)
            inverse0, mean0 = weights(0, cols0, u0, top0)
            cols1, head1, q1, u1, top1 = scores(1)
            grads(0, cols0, head0, q0, u0, inverse0, mean0)
            inverse1, mean1 = weights(1, cols1, u1, top1)
            grads(1, cols1, head1, q1, u1, inverse1, mean1)

        def fold(p, i):
            return KEEP[p, i] + CR[p, i].astype(F32)

        def far_kind(yd):
            return (1 - keep_kind) * 2 + yd

        def near_kind(yd):
            return keep_kind * 2 + yd

        def x1_early(p):
            core_send(p, 4).wait_recv()
            for yd in range(2):
                X1S[p, yd] = fold(p, far_kind(yd)).astype(BF)
            x1_send(p, 2).start()
            for yd in range(2):
                KEEP[p, near_kind(yd)] = fold(p, near_kind(yd))

        def x2_early(p):
            x1_send(p, 2).wait_recv()
            for yd in range(2):
                total = KEEP[p, near_kind(yd)] + X1R[p, yd].astype(F32)
                KEEP[p, near_kind(yd)] = total
                X2S[p, yd] = total.astype(BF)

            @pl.when(x >= 2)
            def _():
                x2_send(p, 2).start()

        def y_early(p):
            @pl.when(x < 2)
            def _():
                x2_send(p, 2).wait_recv()
                YS[p] = (KEEP[p, near_kind(1 - yl)] + X2R[p, 1 - yl].astype(F32)).astype(BF)
                y_send(p).start()
                KEEP[p, near_kind(yl)] = KEEP[p, near_kind(yl)] + X2R[p, yl].astype(F32)

        def z_send(p):
            return rcopy(ZS.at[p - 2], ZR.at[p - 2], z_s.at[p - 2], z_r.at[p - 2], yside)

        def y_late(p):
            core_send(p, 4).wait_recv()
            for kind in range(2):
                ZS[p - 2, kind] = fold(p, 2 * kind + 1 - yl).astype(BF)
            z_send(p).start()
            for kind in range(2):
                KEEP[p, 2 * kind + yl] = fold(p, 2 * kind + yl)

        def x1_late(p):
            z_send(p).wait_recv()
            far = 1 - keep_kind
            X1S[p, 0] = (KEEP[p, far_kind(yl)] + ZR[p - 2, far].astype(F32)).astype(BF)
            x1_send(p, 1).start()
            KEEP[p, near_kind(yl)] = KEEP[p, near_kind(yl)] + ZR[p - 2, keep_kind].astype(F32)

        def x2_late(p):
            x1_send(p, 1).wait_recv()
            total = KEEP[p, near_kind(yl)] + X1R[p, 0].astype(F32)
            KEEP[p, near_kind(yl)] = total
            X2S[p, 0] = total.astype(BF)

            @pl.when(x >= 2)
            def _():
                x2_send(p, 1).start()

        def pair(p):
            for half in range(2):
                q_send(p, half).wait_recv()
            attend(p)
            qg_send(p).start()

        def weigh(p):
            cols = ds(p, BLK)
            weight_part(p, 2, lambda kind: (KG, VG)[kind][:, cols])

        def early_step(p, carry):
            pair(p)

            @pl.when(p == 1)
            def _():
                x1_early(0)

            weigh(p)
            return carry

        def late_step(p, carry):
            pair(p)

            @pl.when(p == 2)
            def _():
                x1_early(1)

            return carry

        lax.fori_loop(0, 2, early_step, 0)
        lax.fori_loop(2, 4, late_step, 0)

        def part(d):
            rows = ds(d, BLK)
            for j in range(4):
                out = pl.ds(j * BLK, BLK)
                PS[d, :, out] = (nt(KG[rows], W[0, out]) + nt(VG[rows], W[1, out])).astype(BF)

        def first():
            weigh(2)
            x2_early(0)
            weigh(3)
            y_late(2)

        input_parts(part, first, lambda: y_late(3), lambda: x2_early(1))
        input_forward()
        y_early(0)
        x1_late(2)
        y_early(1)
        x1_late(3)
        x2_late(2)
        x2_late(3)
        ig[0] = input_total().astype(BF)

        @pl.when(x < 2)
        def _():
            for p in range(2):
                y_send(p).wait_recv()
                wg[0, :, pl.ds(p * BLK, BLK)] = KEEP[p, near_kind(yl)] + YR[p].astype(F32)
            for p in range(2, 4):
                x2_send(p, 1).wait_recv()
                wg[0, :, pl.ds(p * BLK, BLK)] = KEEP[p, near_kind(yl)] + X2R[p, 0].astype(F32)

        @pl.when(x >= 2)
        def _():
            wg[...] = jnp.zeros_like(wg)

        for p in range(4):
            n = 2 if p < 2 else 1
            qg_send(p).wait_send()
            core_send(p, 4).wait_send()
            x1_send(p, n).wait_send()
            if p >= 2:
                z_send(p).wait_send()

        @pl.when(x >= 2)
        def _():
            for p in range(4):
                x2_send(p, 2 if p < 2 else 1).wait_send()

        @pl.when(x < 2)
        def _():
            for p in range(2):
                y_send(p).wait_send()

    @pl.when(is_neural)
    def _():
        tiny = eighth // 2

        def spread(half, d, i, rows):
            s = TOKX.at[(x + 4 - d) % 4, rows]
            device = right if i % 2 == 0 else left
            return rcopy(s, s, ar_s.at[half, d - 1, i], ar_r.at[half, d - 1, i], device)

        def eighth_of(half, b):
            return ds(4 * half + b, eighth)

        def first_of(half, b):
            return ds(8 * half + 2 * b, tiny)

        def second_of(half, b):
            return ds(8 * half + 2 * b + 1, tiny)

        def spread_start(half):
            for d in (1, 3, 2):
                swap_recv(half, d).wait_recv()
                spread(half, d, 0, eighth_of(half, m)).start()
                spread(half, d, 1, eighth_of(half, m)).start()

        def spread_on(half):
            for d in (1, 3, 2):
                spread(half, d, 0, eighth_of(half, left_m)).wait_recv()
                spread(half, d, 2, first_of(half, left_m)).start()
                spread(half, d, 1, eighth_of(half, right_m)).wait_recv()
                spread(half, d, 3, second_of(half, right_m)).start()

        def spread_end():
            for d in (1, 3, 2):
                for half in range(2):
                    spread(half, d, 2, first_of(half, far_m)).wait_recv()
                    spread(half, d, 3, second_of(half, far_m)).wait_recv()
                FT[:, ds((x + 4 - d) % 4, BLK)] = TOKX[(x + 4 - d) % 4].T

        right_x, left_x, far_x = (x + 1) % 4, (x + 3) % 4, (x + 2) % 4

        def gather(p, i, block):
            rows = (ds(block, BLK), ds(block, BLK), ds(2 * block, HALF), ds(2 * block + 1, HALF))[i]
            s = QGX.at[p, rows]
            return rcopy(s, s, xg_s.at[p, i], xg_r.at[p, i], xdev(right_x if i % 2 == 0 else left_x))

        def relay(p):
            qg_send(p).wait_recv()
            gather(p, 0, x).start()
            gather(p, 1, x).start()

        def relay_on(p):
            gather(p, 0, left_x).wait_recv()
            gather(p, 2, left_x).start()
            gather(p, 1, right_x).wait_recv()
            gather(p, 3, right_x).start()

        def chunk(p):
            gather(p, 2, far_x).wait_recv()
            gather(p, 3, far_x).wait_recv()
            weight_part(p, 1, lambda kind: QGX[p])

        def stage_y(p):
            core_send(p, 2).wait_recv()
            YS[p] = (KEEP[p, 1 - yl] + CR[p, 1 - yl].astype(F32)).astype(BF)
            y_send(p).start()
            KEEP[p, yl] = KEEP[p, yl] + CR[p, yl].astype(F32)

        def part(d):
            for j in range(4):
                out = pl.ds(j * BLK, BLK)
                total = None
                for p in range(4):
                    more = nt(QGX[p, ds(x, BLK)], W[d, out, pl.ds(p * BLK, BLK)])
                    total = more if total is None else total + more
                PS[d, :, out] = total.astype(BF)

        for d in (1, 3, 2):
            swap_send(1, d).start()
        spread_start(0)
        FT[:, ds(x, BLK)] = TOK[x].T
        spread_start(1)
        spread_on(0)
        relay(0)
        spread_on(1)
        relay(1)
        relay_on(0)
        relay(2)
        relay_on(1)
        relay(3)

        def third():
            relay_on(3)
            spread_end()
            chunk(0)

        input_parts(part, lambda: relay_on(2), lambda: None, third)
        input_forward()
        stage_y(0)
        for p in range(1, 4):
            chunk(p)
            stage_y(p)
        load_cot.wait()
        ig[0] = (input_total() + COT[...].astype(F32)).astype(BF)
        for p in range(4):
            y_send(p).wait_recv()
            wg[0, :, pl.ds(p * BLK, BLK)] = KEEP[p, yl] + YR[p].astype(F32)
        for p in range(4):
            core_send(p, 2).wait_send()
            y_send(p).wait_send()
            gather(p, 0, x).wait_send()
            gather(p, 1, x).wait_send()
            gather(p, 2, left_x).wait_send()
            gather(p, 3, right_x).wait_send()
            for half in range(2):
                q_send(p, half).wait_send()
        for half in range(2):
            for d in (1, 3, 2):
                swap_send(half, d).wait_send()
                spread(half, d, 0, eighth_of(half, m)).wait_send()
                spread(half, d, 1, eighth_of(half, m)).wait_send()
                spread(half, d, 2, first_of(half, left_m)).wait_send()
                spread(half, d, 3, second_of(half, right_m)).wait_send()

    for half in range(2):
        for i in range(4):
            ring(half, i, m).wait_send()
        ring(half, 4, left_m).wait_send()
        ring(half, 5, right_m).wait_send()
    for i in range(6):
        part_send(i).wait_send()


def local(tokens, proj, cotangent, counts, frames):
    vmem = pltpu.VMEM
    dma = pltpu.SemaphoreType.DMA
    scratch = [
        vmem((4, BLK, WIDE), BF),
        vmem((4, WIDE, WIDE), BF),
        vmem((BLK, WIDE), BF),
        vmem((BLK, WIDE), F32),
        vmem((4, BLK, BLK), BF),
        vmem((4, BLK, BLK), BF),
        vmem((BLK, BLK), F32),
        vmem((WIDE, WIDE), BF),
        vmem((WIDE, WIDE), BF),
        vmem((WIDE, WIDE), BF),
        vmem((8, BLK, BLK), F32),
        vmem((8, BLK, BLK), F32),
        vmem((WIDE, WIDE), BF),
        vmem((WIDE, WIDE), BF),
        vmem((4, BLK, BLK), BF),
        vmem((WIDE, WIDE), BF),
        vmem((4, BLK, WIDE), BF),
        vmem((4, WIDE, BLK), BF),
        vmem((4, 4, BLK, BLK), BF),
        vmem((4, 4, BLK, BLK), BF),
        vmem((4, 4, BLK, BLK), F32),
        vmem((4, 2, BLK, BLK), BF),
        vmem((4, 2, BLK, BLK), BF),
        vmem((4, 2, BLK, BLK), BF),
        vmem((4, 2, BLK, BLK), BF),
        vmem((4, BLK, BLK), BF),
        vmem((4, BLK, BLK), BF),
        vmem((2, 2, BLK, BLK), BF),
        vmem((2, 2, BLK, BLK), BF),
        vmem((4, BLK, WIDE), BF),
        vmem((HALF, WIDE), BF),
        vmem((HALF, WIDE), BF),
        vmem((BLK, WIDE), BF),
        vmem((BLK, WIDE), BF),
        dma((6,)),
        dma((2, 6)), dma((2, 6)),
        dma((4, 2)), dma((4, 2)),
        dma((4,)), dma((4,)),
        dma((2, 3)), dma((2, 3)),
        dma((2, 3, 4)), dma((2, 3, 4)),
        dma((4, 4)), dma((4, 4)),
        dma((4,)), dma((4,)),
        dma((4,)), dma((4,)),
        dma((4,)), dma((4,)),
        dma((4,)), dma((4,)),
        dma((2,)), dma((2,)),
        dma((6,)), dma((6,)),
    ]
    anywhere = pl.BlockSpec(memory_space=pl.ANY)
    in_vmem = pl.BlockSpec(memory_space=vmem)
    return pl.pallas_call(
        kernel,
        out_shape=(
            jax.ShapeDtypeStruct((1, BLK, WIDE), BF),
            jax.ShapeDtypeStruct((1, BLK, WIDE), F32),
        ),
        in_specs=[
            anywhere, anywhere, anywhere,
            pl.BlockSpec(memory_space=pltpu.SMEM),
            in_vmem,
        ],
        out_specs=(in_vmem, in_vmem),
        scratch_shapes=scratch,
        compiler_params=pltpu.CompilerParams(
            collective_id=0, has_side_effects=True, vmem_limit_bytes=60 * 2**20
        ),
        cost_estimate=pl.CostEstimate(
            flops=20 * 10**9, bytes_accessed=16 * 2**20, transcendentals=2**21
        ),
    )(tokens, proj, cotangent, counts, frames.reshape(1, BLK))


def solution(mesh):
    return jax.shard_map(
        local,
        mesh=mesh,
        in_specs=(
            P("group", "win", "mp"),
            P("group", None, "mp"),
            P("win", "mp"),
            P("win"),
            P("win"),
        ),
        out_specs=(P("group", "win", "mp"), P("group", "win", "mp")),
        check_vma=False,
    )
```

```python
import jax
import jax.numpy as jnp
from jax import lax
from jax.experimental import pallas as pl
from jax.experimental.pallas import tpu as pltpu
from jax.sharding import PartitionSpec as P

MESH = pl.DeviceIdType.MESH
BF = jnp.bfloat16
F32 = jnp.float32
FACTOR = 128 ** (-0.5)
LOG2_E = 1.4426950408889634
BLK = 256
WIDE = 1024
HALF = 128
PIECE = 64


def nn(a, b):
    return jnp.dot(a, b, preferred_element_type=F32)


def nt(a, b):
    return lax.dot_general(a, b, (((1,), (1,)), ((), ())), preferred_element_type=F32)


def tn(a, b):
    return lax.dot_general(a, b, (((0,), (0,)), ((), ())), preferred_element_type=F32)


def ds(i, size):
    return pl.ds(pl.multiple_of(i * size, size), size)


def rcopy(src, dst, send_sem, recv_sem, device):
    return pltpu.make_async_remote_copy(
        src_ref=src,
        dst_ref=dst,
        send_sem=send_sem,
        recv_sem=recv_sem,
        device_id=device,
        device_id_type=MESH,
    )


def kernel(
    tok, proj, cot, counts, frames, ig, wg,
    TOK, W, COT, ACC, Q, U, BIAS, K, KT, V, S, DP, KG, VG, QG, FT, TOKX, QGX,
    CS, CR, KEEP, X1S, X1R, X2S, X2R, YS, YR, ZS, ZR, PS, RAL, RAR, RBL, RBR,
    l_sem, ag_s, ag_r, q_s, q_r, qg_s, qg_r, aa_s, aa_r, ar_s, ar_r, xg_s, xg_r,
    cs_s, cs_r, x1_s, x1_r, x2_s, x2_r, y_s, y_r, z_s, z_r, rs_s, rs_r,
):
    g = lax.axis_index("group")
    w = lax.axis_index("win")
    m = lax.axis_index("mp")
    x = w // 4
    yl = (w // 2) % 2
    c = w % 2
    is_video = g == 0
    is_neural = g == 1
    right_m, left_m, far_m = (m + 1) % 4, (m + 3) % 4, (m + 2) % 4
    right, left = {"mp": right_m}, {"mp": left_m}
    partner = {"group": 1 - g}
    core = {"win": w + 1 - 2 * c}
    yside = {"win": w + 2 - 4 * yl}

    def xdev(xp):
        return {"win": xp * 4 + w % 4}

    xnear = xdev(x + 1 - 2 * (x % 2))
    xback = xdev(3 - x)
    keep_kind = ((x + 1) // 2) % 2

    load_tok = pltpu.make_async_copy(tok.at[0], TOK.at[m], l_sem.at[0])
    load_tok.start()
    load_cot = pltpu.make_async_copy(cot, COT, l_sem.at[1])

    def load_w(i, b):
        return pltpu.make_async_copy(proj.at[0, ds(b, WIDE)], W.at[b], l_sem.at[2 + i])

    order = (m, left_m, right_m, far_m)

    @pl.when(is_neural)
    def _():
        for i in range(4):
            load_w(i, order[i]).start()

    @pl.when(is_video)
    def _():
        for i in range(2):
            load_w(i, i).start()

    load_cot.start()

    barrier = pltpu.get_barrier_semaphore()
    greet = [right, left, partner, core, yside] + [xdev((x + d) % 4) for d in (1, 2, 3)]
    for device in greet:
        pl.semaphore_signal(barrier, inc=1, device_id=device, device_id_type=MESH)
    pl.semaphore_wait(barrier, len(greet))

    lo, hi = pl.ds(0, HALF), pl.ds(HALF, HALF)

    def ring(half, i, block):
        device = right if i in (0, 1, 4) else left
        start = half * HALF + (0 if i in (0, 3, 4) else PIECE)
        rows = pl.ds(start, PIECE)
        return rcopy(TOK.at[block, rows], TOK.at[block, rows], ag_s.at[half, i], ag_r.at[half, i], device)

    def ring_start(half):
        for i in (0, 2, 1, 3):
            ring(half, i, m).start()

    def ring_forward(half):
        ring(half, 0, left_m).wait_recv()
        ring(half, 4, left_m).start()
        ring(half, 2, right_m).wait_recv()
        ring(half, 5, right_m).start()

    def q_send(j, half):
        s = Q.at[j, pl.ds(half * HALF, HALF)]
        return rcopy(s, s, q_s.at[j, half], q_r.at[j, half], partner)

    def project(b, i, half):
        rows = pl.ds(half * HALF, HALF)

        @pl.when(is_video)
        def _():
            if i == 0 and half == 0:
                load_w(0, 0).wait()
                load_w(1, 1).wait()
            keys = ds(2 * b + half, HALF)
            for j in range(4):
                cols = pl.ds(j * BLK, BLK)
                K[keys, cols] = nn(TOK[b, rows], W[0, :, cols]).astype(BF)
                V[keys, cols] = nn(TOK[b, rows], W[1, :, cols]).astype(BF)
            FT[:, keys] = TOK[b, rows].T
            KT[:, keys] = K[keys].T

        @pl.when(is_neural)
        def _():
            if half == 0:
                load_w(i, b).wait()
            for j in range(4):
                cols = pl.ds(j * BLK, BLK)
                part = nn(TOK[b, rows], W[b, :, cols])
                if i == 0:
                    ACC[rows, cols] = part
                elif i < 3:
                    ACC[rows, cols] += part
                else:
                    Q[j, rows] = (ACC[rows, cols] + part).astype(BF)
                    q_send(j, half).start()

    eighth = HALF // 4

    def swap_send(half, d):
        rows = ds(4 * half + m, eighth)
        return rcopy(
            TOK.at[(x + d) % 4, rows], TOKX.at[x, rows],
            aa_s.at[half, d - 1], aa_r.at[half, d - 1], xdev((x + d) % 4),
        )

    def swap_recv(half, d):
        s = TOKX.at[(x + 4 - d) % 4, ds(4 * half + m, eighth)]
        return rcopy(s, s, aa_s.at[half, d - 1], aa_r.at[half, d - 1], xdev((x + d) % 4))

    load_tok.wait()
    ring_start(0)
    project(m, 0, 0)
    ring_forward(0)
    ring_start(1)
    ring(0, 1, left_m).wait_recv()
    project(left_m, 1, 0)
    ring(0, 3, right_m).wait_recv()
    project(right_m, 2, 0)
    ring(0, 4, far_m).wait_recv()
    ring(0, 5, far_m).wait_recv()
    project(far_m, 3, 0)

    @pl.when(is_neural)
    def _():
        for d in (1, 3, 2):
            swap_send(0, d).start()

    project(m, 0, 1)
    ring_forward(1)
    ring(1, 1, left_m).wait_recv()
    project(left_m, 1, 1)
    ring(1, 3, right_m).wait_recv()
    project(right_m, 2, 1)

    @pl.when(is_video)
    def _():
        load_cot.wait()
        live = lax.broadcasted_iota(jnp.int32, (BLK, BLK), 0) < counts[0]
        for j in range(4):
            part = COT[:, pl.ds(j * BLK, BLK)].astype(F32)
            U[j] = jnp.where(live, part, jnp.zeros_like(part)).astype(BF)
        key_frame = lax.broadcasted_iota(jnp.int32, (BLK, BLK), 0) >> 6
        BIAS[...] = jnp.where(key_frame <= frames[...], 0.0, -1e30).astype(F32)

    ring(1, 4, far_m).wait_recv()
    ring(1, 5, far_m).wait_recv()
    project(far_m, 3, 1)

    def core_send(p, count):
        return rcopy(CS.at[p, pl.ds(0, count)], CR.at[p, pl.ds(0, count)], cs_s.at[p], cs_r.at[p], core)

    def weight_part(p, kinds, rhs):
        for kind in range(kinds):
            for yd in range(2):
                CS[p, kind * 2 + yd] = nn(FT[ds(2 * yd + 1 - c, BLK)], rhs(kind)).astype(BF)
        core_send(p, 2 * kinds).start()
        for kind in range(kinds):
            for yd in range(2):
                KEEP[p, kind * 2 + yd] = nn(FT[ds(2 * yd + c, BLK)], rhs(kind))

    def y_send(p):
        return rcopy(YS.at[p], YR.at[p], y_s.at[p], y_r.at[p], yside)

    def x1_send(p, n):
        some = pl.ds(0, n)
        return rcopy(X1S.at[p, some], X1R.at[p, some], x1_s.at[p], x1_r.at[p], xnear)

    def x2_send(p, n):
        some = pl.ds(0, n)
        return rcopy(X2S.at[p, some], X2R.at[p, some], x2_s.at[p], x2_r.at[p], xback)

    def part_send(i):
        src = (
            PS.at[far_m, lo], PS.at[right_m, hi], PS.at[right_m, lo],
            PS.at[far_m, hi], PS.at[left_m, lo], PS.at[left_m, hi],
        )[i]
        dst = (RAL, RBL.at[hi], RBL.at[lo], RAR, RBR.at[lo], RBR.at[hi])[i]
        return rcopy(src, dst, rs_s.at[i], rs_r.at[i], right if i < 3 else left)

    def input_parts(part, first, second, third):
        part(far_m)
        part_send(0).start()
        part_send(3).start()
        first()
        part(right_m)
        part_send(1).start()
        part(left_m)
        part_send(4).start()
        second()
        part(m)
        third()

    def input_forward():
        part_send(0).wait_recv()
        PS[right_m, lo] = (PS[right_m, lo].astype(F32) + RAL[...].astype(F32)).astype(BF)
        part_send(2).start()
        part_send(3).wait_recv()
        PS[left_m, hi] = (PS[left_m, hi].astype(F32) + RAR[...].astype(F32)).astype(BF)
        part_send(5).start()

    def input_total():
        for i in (1, 2, 4, 5):
            part_send(i).wait_recv()
        return PS[m].astype(F32) + RBL[...].astype(F32) + RBR[...].astype(F32)

    def qg_send(p):
        return rcopy(QG.at[p], QGX.at[p, ds(x, BLK)], qg_s.at[p], qg_r.at[p], partner)

    @pl.when(is_video)
    def _():
        def attend(p):
            blocks = [pl.ds(t * BLK, BLK) for t in range(4)]

            def scores(hh):
                cols = ds(2 * p + hh, HALF)
                head = pl.ds(hh * HALF, HALF)
                q = Q[p, :, head]
                u = U[p, :, head]
                q_t = q.T
                top = None
                for t in range(4):
                    s = nn(K[blocks[t], cols], q_t) + BIAS[...]
                    S[4 * hh + t] = s
                    high = jnp.max(s, axis=0, keepdims=True)
                    top = high if top is None else jnp.maximum(top, high)
                return cols, head, q, u, top

            def weights(hh, cols, u, top):
                u_t = u.T
                total = jnp.zeros_like(top)
                weighted = jnp.zeros_like(top)
                for t in range(4):
                    e = jnp.exp2((S[4 * hh + t] - top) * (FACTOR * LOG2_E))
                    d = nn(V[blocks[t], cols], u_t)
                    S[4 * hh + t] = e
                    DP[4 * hh + t] = d
                    total += jnp.sum(e, axis=0, keepdims=True)
                    weighted += jnp.sum(e * d, axis=0, keepdims=True)
                inverse = 1.0 / total
                return inverse, weighted * inverse

            def grads(hh, cols, head, q, u, inverse, mean):
                query_grad = None
                for t in range(4):
                    a = S[4 * hh + t] * inverse
                    VG[blocks[t], cols] = nn(a.astype(BF), u).astype(BF)
                    sg = (a * (DP[4 * hh + t] - mean) * FACTOR).astype(BF)
                    KG[blocks[t], cols] = nn(sg, q).astype(BF)
                    more = nn(KT[cols, blocks[t]], sg)
                    query_grad = more if query_grad is None else query_grad + more
                QG[p, :, head] = query_grad.T.astype(BF)

            cols0, head0, q0, u0, top0 = scores(0)
            inverse0, mean0 = weights(0, cols0, u0, top0)
            cols1, head1, q1, u1, top1 = scores(1)
            grads(0, cols0, head0, q0, u0, inverse0, mean0)
            inverse1, mean1 = weights(1, cols1, u1, top1)
            grads(1, cols1, head1, q1, u1, inverse1, mean1)

        def fold(p, i):
            return KEEP[p, i] + CR[p, i].astype(F32)

        def far_kind(yd):
            return (1 - keep_kind) * 2 + yd

        def near_kind(yd):
            return keep_kind * 2 + yd

        def x1_early(p):
            core_send(p, 4).wait_recv()
            for yd in range(2):
                X1S[p, yd] = fold(p, far_kind(yd)).astype(BF)
            x1_send(p, 2).start()
            for yd in range(2):
                KEEP[p, near_kind(yd)] = fold(p, near_kind(yd))

        def x2_early(p):
            x1_send(p, 2).wait_recv()
            for yd in range(2):
                total = KEEP[p, near_kind(yd)] + X1R[p, yd].astype(F32)
                KEEP[p, near_kind(yd)] = total
                X2S[p, yd] = total.astype(BF)

            @pl.when(x >= 2)
            def _():
                x2_send(p, 2).start()

        def y_early(p):
            @pl.when(x < 2)
            def _():
                x2_send(p, 2).wait_recv()
                YS[p] = (KEEP[p, near_kind(1 - yl)] + X2R[p, 1 - yl].astype(F32)).astype(BF)
                y_send(p).start()
                KEEP[p, near_kind(yl)] = KEEP[p, near_kind(yl)] + X2R[p, yl].astype(F32)

        def z_send(p, kind):
            return rcopy(
                ZS.at[p - 2, kind], ZR.at[p - 2, kind], z_s.at[p - 2, kind], z_r.at[p - 2, kind], yside
            )

        far = 1 - keep_kind

        def y_late(p):
            core_send(p, 4).wait_recv()
            for kind in (far, keep_kind):
                ZS[p - 2, kind] = fold(p, 2 * kind + 1 - yl).astype(BF)
                z_send(p, kind).start()
            for kind in range(2):
                KEEP[p, 2 * kind + yl] = fold(p, 2 * kind + yl)

        def x1_late(p):
            z_send(p, far).wait_recv()
            X1S[p, 0] = (KEEP[p, far_kind(yl)] + ZR[p - 2, far].astype(F32)).astype(BF)
            x1_send(p, 1).start()

        def x2_late(p):
            z_send(p, keep_kind).wait_recv()
            x1_send(p, 1).wait_recv()
            total = KEEP[p, near_kind(yl)] + ZR[p - 2, keep_kind].astype(F32) + X1R[p, 0].astype(F32)
            KEEP[p, near_kind(yl)] = total
            X2S[p, 0] = total.astype(BF)

            @pl.when(x >= 2)
            def _():
                x2_send(p, 1).start()

        def pair(p):
            for half in range(2):
                q_send(p, half).wait_recv()
            attend(p)
            qg_send(p).start()

        def weigh(p):
            cols = ds(p, BLK)
            weight_part(p, 2, lambda kind: (KG, VG)[kind][:, cols])

        def step(p, carry):
            pair(p)

            @pl.when(p == 0)
            def _():
                weigh(0)

            @pl.when(p == 1)
            def _():
                x1_early(0)

            return carry

        lax.fori_loop(0, 4, step, 0)

        def part(d):
            rows = ds(d, BLK)
            for j in range(4):
                out = pl.ds(j * BLK, BLK)
                PS[d, :, out] = (nt(KG[rows], W[0, out]) + nt(VG[rows], W[1, out])).astype(BF)

        def first():
            x2_early(0)
            weigh(1)
            weigh(2)
            x1_early(1)
            weigh(3)
            y_late(2)

        input_parts(part, first, lambda: y_late(3), lambda: y_early(0))
        input_forward()
        x1_late(2)
        x2_early(1)
        x1_late(3)
        x2_late(2)
        y_early(1)
        x2_late(3)
        ig[0] = input_total().astype(BF)

        @pl.when(x < 2)
        def _():
            for p in range(2):
                y_send(p).wait_recv()
                wg[0, :, pl.ds(p * BLK, BLK)] = KEEP[p, near_kind(yl)] + YR[p].astype(F32)
            for p in range(2, 4):
                x2_send(p, 1).wait_recv()
                wg[0, :, pl.ds(p * BLK, BLK)] = KEEP[p, near_kind(yl)] + X2R[p, 0].astype(F32)

        @pl.when(x >= 2)
        def _():
            wg[...] = jnp.zeros_like(wg)

        for p in range(4):
            n = 2 if p < 2 else 1
            qg_send(p).wait_send()
            core_send(p, 4).wait_send()
            x1_send(p, n).wait_send()
            if p >= 2:
                z_send(p, 0).wait_send()
                z_send(p, 1).wait_send()

        @pl.when(x >= 2)
        def _():
            for p in range(4):
                x2_send(p, 2 if p < 2 else 1).wait_send()

        @pl.when(x < 2)
        def _():
            for p in range(2):
                y_send(p).wait_send()

    @pl.when(is_neural)
    def _():
        tiny = eighth // 2

        def spread(half, d, i, rows):
            s = TOKX.at[(x + 4 - d) % 4, rows]
            device = right if i % 2 == 0 else left
            return rcopy(s, s, ar_s.at[half, d - 1, i], ar_r.at[half, d - 1, i], device)

        def eighth_of(half, b):
            return ds(4 * half + b, eighth)

        def first_of(half, b):
            return ds(8 * half + 2 * b, tiny)

        def second_of(half, b):
            return ds(8 * half + 2 * b + 1, tiny)

        def spread_start(half):
            for d in (1, 3, 2):
                swap_recv(half, d).wait_recv()
                spread(half, d, 0, eighth_of(half, m)).start()
                spread(half, d, 1, eighth_of(half, m)).start()

        def spread_on(half):
            for d in (1, 3, 2):
                spread(half, d, 0, eighth_of(half, left_m)).wait_recv()
                spread(half, d, 2, first_of(half, left_m)).start()
                spread(half, d, 1, eighth_of(half, right_m)).wait_recv()
                spread(half, d, 3, second_of(half, right_m)).start()

        def spread_end():
            for d in (1, 3, 2):
                for half in range(2):
                    spread(half, d, 2, first_of(half, far_m)).wait_recv()
                    spread(half, d, 3, second_of(half, far_m)).wait_recv()
                FT[:, ds((x + 4 - d) % 4, BLK)] = TOKX[(x + 4 - d) % 4].T

        right_x, left_x, far_x = (x + 1) % 4, (x + 3) % 4, (x + 2) % 4

        def gather(p, i, block):
            rows = (ds(block, BLK), ds(block, BLK), ds(2 * block, HALF), ds(2 * block + 1, HALF))[i]
            s = QGX.at[p, rows]
            return rcopy(s, s, xg_s.at[p, i], xg_r.at[p, i], xdev(right_x if i % 2 == 0 else left_x))

        def relay(p):
            qg_send(p).wait_recv()
            gather(p, 0, x).start()
            gather(p, 1, x).start()

        def relay_on(p):
            gather(p, 0, left_x).wait_recv()
            gather(p, 2, left_x).start()
            gather(p, 1, right_x).wait_recv()
            gather(p, 3, right_x).start()

        def chunk(p):
            gather(p, 2, far_x).wait_recv()
            gather(p, 3, far_x).wait_recv()
            weight_part(p, 1, lambda kind: QGX[p])

        def stage_y(p):
            core_send(p, 2).wait_recv()
            YS[p] = (KEEP[p, 1 - yl] + CR[p, 1 - yl].astype(F32)).astype(BF)
            y_send(p).start()
            KEEP[p, yl] = KEEP[p, yl] + CR[p, yl].astype(F32)

        def part(d):
            for j in range(4):
                out = pl.ds(j * BLK, BLK)
                total = None
                for p in range(4):
                    more = nt(QGX[p, ds(x, BLK)], W[d, out, pl.ds(p * BLK, BLK)])
                    total = more if total is None else total + more
                PS[d, :, out] = total.astype(BF)

        for d in (1, 3, 2):
            swap_send(1, d).start()
        spread_start(0)
        FT[:, ds(x, BLK)] = TOK[x].T
        spread_start(1)
        spread_on(0)
        relay(0)
        spread_on(1)
        relay(1)
        relay_on(0)
        relay(2)
        relay_on(1)
        spread_end()
        chunk(0)
        relay(3)

        def third():
            stage_y(0)
            relay_on(2)
            chunk(1)
            relay_on(3)

        input_parts(part, lambda: None, lambda: None, third)
        input_forward()
        stage_y(1)
        for p in range(2, 4):
            chunk(p)
            stage_y(p)
        load_cot.wait()
        ig[0] = (input_total() + COT[...].astype(F32)).astype(BF)
        for p in range(4):
            y_send(p).wait_recv()
            wg[0, :, pl.ds(p * BLK, BLK)] = KEEP[p, yl] + YR[p].astype(F32)
        for p in range(4):
            core_send(p, 2).wait_send()
            y_send(p).wait_send()
            gather(p, 0, x).wait_send()
            gather(p, 1, x).wait_send()
            gather(p, 2, left_x).wait_send()
            gather(p, 3, right_x).wait_send()
            for half in range(2):
                q_send(p, half).wait_send()
        for half in range(2):
            for d in (1, 3, 2):
                swap_send(half, d).wait_send()
                spread(half, d, 0, eighth_of(half, m)).wait_send()
                spread(half, d, 1, eighth_of(half, m)).wait_send()
                spread(half, d, 2, first_of(half, left_m)).wait_send()
                spread(half, d, 3, second_of(half, right_m)).wait_send()

    for half in range(2):
        for i in range(4):
            ring(half, i, m).wait_send()
        ring(half, 4, left_m).wait_send()
        ring(half, 5, right_m).wait_send()
    for i in range(6):
        part_send(i).wait_send()


def local(tokens, proj, cotangent, counts, frames):
    vmem = pltpu.VMEM
    dma = pltpu.SemaphoreType.DMA
    scratch = [
        vmem((4, BLK, WIDE), BF),
        vmem((4, WIDE, WIDE), BF),
        vmem((BLK, WIDE), BF),
        vmem((BLK, WIDE), F32),
        vmem((4, BLK, BLK), BF),
        vmem((4, BLK, BLK), BF),
        vmem((BLK, BLK), F32),
        vmem((WIDE, WIDE), BF),
        vmem((WIDE, WIDE), BF),
        vmem((WIDE, WIDE), BF),
        vmem((8, BLK, BLK), F32),
        vmem((8, BLK, BLK), F32),
        vmem((WIDE, WIDE), BF),
        vmem((WIDE, WIDE), BF),
        vmem((4, BLK, BLK), BF),
        vmem((WIDE, WIDE), BF),
        vmem((4, BLK, WIDE), BF),
        vmem((4, WIDE, BLK), BF),
        vmem((4, 4, BLK, BLK), BF),
        vmem((4, 4, BLK, BLK), BF),
        vmem((4, 4, BLK, BLK), F32),
        vmem((4, 2, BLK, BLK), BF),
        vmem((4, 2, BLK, BLK), BF),
        vmem((4, 2, BLK, BLK), BF),
        vmem((4, 2, BLK, BLK), BF),
        vmem((4, BLK, BLK), BF),
        vmem((4, BLK, BLK), BF),
        vmem((2, 2, BLK, BLK), BF),
        vmem((2, 2, BLK, BLK), BF),
        vmem((4, BLK, WIDE), BF),
        vmem((HALF, WIDE), BF),
        vmem((HALF, WIDE), BF),
        vmem((BLK, WIDE), BF),
        vmem((BLK, WIDE), BF),
        dma((6,)),
        dma((2, 6)), dma((2, 6)),
        dma((4, 2)), dma((4, 2)),
        dma((4,)), dma((4,)),
        dma((2, 3)), dma((2, 3)),
        dma((2, 3, 4)), dma((2, 3, 4)),
        dma((4, 4)), dma((4, 4)),
        dma((4,)), dma((4,)),
        dma((4,)), dma((4,)),
        dma((4,)), dma((4,)),
        dma((4,)), dma((4,)),
        dma((2, 2)), dma((2, 2)),
        dma((6,)), dma((6,)),
    ]
    anywhere = pl.BlockSpec(memory_space=pl.ANY)
    in_vmem = pl.BlockSpec(memory_space=vmem)
    return pl.pallas_call(
        kernel,
        out_shape=(vmem((1, BLK, WIDE), BF), vmem((1, BLK, WIDE), F32)),
        in_specs=[
            anywhere, anywhere, anywhere,
            pl.BlockSpec(memory_space=pltpu.SMEM),
            in_vmem,
        ],
        out_specs=(in_vmem, in_vmem),
        scratch_shapes=scratch,
        compiler_params=pltpu.CompilerParams(
            collective_id=0, has_side_effects=True, vmem_limit_bytes=56 * 2**20
        ),
        cost_estimate=pl.CostEstimate(
            flops=20 * 10**9, bytes_accessed=16 * 2**20, transcendentals=2**21
        ),
    )(tokens, proj, cotangent, counts, frames.reshape(1, BLK))


def solution(mesh):
    return jax.shard_map(
        local,
        mesh=mesh,
        in_specs=(
            P("group", "win", "mp"),
            P("group", None, "mp"),
            P("win", "mp"),
            P("win"),
            P("win"),
        ),
        out_specs=(P("group", "win", "mp"), P("group", "win", "mp")),
        check_vma=False,
    )
```

```python
import jax
import jax.numpy as jnp
from jax import lax
from jax.experimental import pallas as pl
from jax.experimental.pallas import tpu as pltpu
from jax.sharding import PartitionSpec as P

MESH = pl.DeviceIdType.MESH
BF = jnp.bfloat16
F32 = jnp.float32
FACTOR = 128 ** (-0.5)
LOG2_E = 1.4426950408889634
BLK = 256
WIDE = 1024
HALF = 128
PIECE = 64


def nn(a, b):
    return jnp.dot(a, b, preferred_element_type=F32)


def nt(a, b):
    return lax.dot_general(a, b, (((1,), (1,)), ((), ())), preferred_element_type=F32)


def tn(a, b):
    return lax.dot_general(a, b, (((0,), (0,)), ((), ())), preferred_element_type=F32)


def ds(i, size):
    return pl.ds(pl.multiple_of(i * size, size), size)


def rcopy(src, dst, send_sem, recv_sem, device):
    return pltpu.make_async_remote_copy(
        src_ref=src,
        dst_ref=dst,
        send_sem=send_sem,
        recv_sem=recv_sem,
        device_id=device,
        device_id_type=MESH,
    )


def kernel(
    tok, proj, cot, counts_hbm, frames_hbm, ig, wg,
    counts, frames, TOK, W, COT, ACC, Q, U, BIAS, K, KT, V, S, DP, GR, QG, FT, TOKX, QGX,
    CS, CR, KEEP, X1S, X1R, X2S, X2R, YS, YR, ZS, ZR, PS, RAL, RAR, RBL, RBR,
    l_sem, ag_s, ag_r, q_s, q_r, qg_s, qg_r, aa_s, aa_r, ar_s, ar_r, xg_s, xg_r,
    cs_s, cs_r, x1_s, x1_r, x2_s, x2_r, y_s, y_r, z_s, z_r, rs_s, rs_r,
):
    g = lax.axis_index("group")
    w = lax.axis_index("win")
    m = lax.axis_index("mp")
    x = w // 4
    yl = (w // 2) % 2
    c = w % 2
    is_video = g == 0
    is_neural = g == 1
    right_m, left_m, far_m = (m + 1) % 4, (m + 3) % 4, (m + 2) % 4
    right, left = {"mp": right_m}, {"mp": left_m}
    partner = {"group": 1 - g}
    core = {"win": w + 1 - 2 * c}
    yside = {"win": w + 2 - 4 * yl}

    def xdev(xp):
        return {"win": xp * 4 + w % 4}

    xnear = xdev(x + 1 - 2 * (x % 2))
    xback = xdev(3 - x)
    keep_kind = ((x + 1) // 2) % 2

    load_tok = pltpu.make_async_copy(tok.at[0], TOK.at[m], l_sem.at[0])
    load_tok.start()
    load_cot = pltpu.make_async_copy(cot, COT, l_sem.at[1])

    def load_w(i, b):
        return pltpu.make_async_copy(proj.at[0, ds(b, WIDE)], W.at[b], l_sem.at[2 + i])

    order = (m, left_m, right_m, far_m)

    @pl.when(is_neural)
    def _():
        for i in range(4):
            load_w(i, order[i]).start()

    @pl.when(is_video)
    def _():
        for i in range(2):
            load_w(i, i).start()

    load_cot.start()
    load_counts = pltpu.make_async_copy(counts_hbm, counts, l_sem.at[6])
    load_frames = pltpu.make_async_copy(frames_hbm, frames, l_sem.at[7])
    load_counts.start()
    load_frames.start()

    barrier = pltpu.get_barrier_semaphore()
    greet = [right, left, partner, core, yside] + [xdev((x + d) % 4) for d in (1, 2, 3)]
    for device in greet:
        pl.semaphore_signal(barrier, inc=1, device_id=device, device_id_type=MESH)
    pl.semaphore_wait(barrier, len(greet))

    lo, hi = pl.ds(0, HALF), pl.ds(HALF, HALF)

    def ring(half, i, block):
        device = right if i in (0, 1, 4) else left
        start = half * HALF + (0 if i in (0, 3, 4) else PIECE)
        rows = pl.ds(start, PIECE)
        return rcopy(TOK.at[block, rows], TOK.at[block, rows], ag_s.at[half, i], ag_r.at[half, i], device)

    def ring_start(half):
        for i in (0, 2, 1, 3):
            ring(half, i, m).start()

    def ring_forward(half):
        ring(half, 0, left_m).wait_recv()
        ring(half, 4, left_m).start()
        ring(half, 2, right_m).wait_recv()
        ring(half, 5, right_m).start()

    def q_send(j, half):
        s = Q.at[j, pl.ds(half * HALF, HALF)]
        return rcopy(s, s, q_s.at[j, half], q_r.at[j, half], partner)

    def project(b, i, half):
        rows = pl.ds(half * HALF, HALF)

        @pl.when(is_video)
        def _():
            if i == 0 and half == 0:
                load_w(0, 0).wait()
                load_w(1, 1).wait()
            keys = ds(2 * b + half, HALF)
            for j in range(4):
                cols = pl.ds(j * BLK, BLK)
                K[keys, cols] = nn(TOK[b, rows], W[0, :, cols]).astype(BF)
                V[keys, cols] = nn(TOK[b, rows], W[1, :, cols]).astype(BF)
            FT[:, keys] = TOK[b, rows].T
            KT[:, keys] = K[keys].T

        @pl.when(is_neural)
        def _():
            if half == 0:
                load_w(i, b).wait()
            for j in range(4):
                cols = pl.ds(j * BLK, BLK)
                part = nn(TOK[b, rows], W[b, :, cols])
                if i == 0:
                    ACC[rows, cols] = part
                elif i < 3:
                    ACC[rows, cols] += part
                else:
                    Q[j, rows] = (ACC[rows, cols] + part).astype(BF)
                    q_send(j, half).start()

    eighth = HALF // 4

    def swap_send(half, d):
        rows = ds(4 * half + m, eighth)
        return rcopy(
            TOK.at[(x + d) % 4, rows], TOKX.at[x, rows],
            aa_s.at[half, d - 1], aa_r.at[half, d - 1], xdev((x + d) % 4),
        )

    def swap_recv(half, d):
        s = TOKX.at[(x + 4 - d) % 4, ds(4 * half + m, eighth)]
        return rcopy(s, s, aa_s.at[half, d - 1], aa_r.at[half, d - 1], xdev((x + d) % 4))

    load_tok.wait()
    ring_start(0)
    project(m, 0, 0)
    ring_forward(0)
    ring_start(1)
    ring(0, 1, left_m).wait_recv()
    project(left_m, 1, 0)
    ring(0, 3, right_m).wait_recv()
    project(right_m, 2, 0)
    ring(0, 4, far_m).wait_recv()
    ring(0, 5, far_m).wait_recv()
    project(far_m, 3, 0)

    @pl.when(is_neural)
    def _():
        for d in (1, 3, 2):
            swap_send(0, d).start()

    project(m, 0, 1)
    ring_forward(1)
    ring(1, 1, left_m).wait_recv()
    project(left_m, 1, 1)
    ring(1, 3, right_m).wait_recv()
    project(right_m, 2, 1)

    load_counts.wait()
    load_frames.wait()

    @pl.when(is_video)
    def _():
        load_cot.wait()
        live = lax.broadcasted_iota(jnp.int32, (BLK, BLK), 0) < counts[0]
        for j in range(4):
            part = COT[:, pl.ds(j * BLK, BLK)].astype(F32)
            U[j] = jnp.where(live, part, jnp.zeros_like(part)).astype(BF)
        key_frame = lax.broadcasted_iota(jnp.int32, (BLK, BLK), 0) >> 6
        BIAS[...] = jnp.where(key_frame <= frames[...], 0.0, -1e30).astype(F32)

    ring(1, 4, far_m).wait_recv()
    ring(1, 5, far_m).wait_recv()
    project(far_m, 3, 1)

    def core_send(p, kind):
        both = pl.ds(2 * kind, 2)
        return rcopy(CS.at[p, both], CR.at[p, both], cs_s.at[p, kind], cs_r.at[p, kind], core)

    def weight_part(p, kind, rhs):
        for yd in range(2):
            CS[p, kind * 2 + yd] = nn(FT[ds(2 * yd + 1 - c, BLK)], rhs).astype(BF)
        core_send(p, kind).start()
        for yd in range(2):
            KEEP[p, kind * 2 + yd] = nn(FT[ds(2 * yd + c, BLK)], rhs)

    def y_send(p):
        return rcopy(YS.at[p], YR.at[p], y_s.at[p], y_r.at[p], yside)

    def x1_send(p, i):
        return rcopy(X1S.at[p, i], X1R.at[p, i], x1_s.at[p, i], x1_r.at[p, i], xnear)

    def x2_send(p, i):
        return rcopy(X2S.at[p, i], X2R.at[p, i], x2_s.at[p, i], x2_r.at[p, i], xback)

    def part_send(i):
        src = (
            PS.at[far_m, lo], PS.at[right_m, hi], PS.at[right_m, lo],
            PS.at[far_m, hi], PS.at[left_m, lo], PS.at[left_m, hi],
        )[i]
        dst = (RAL, RBL.at[hi], RBL.at[lo], RAR, RBR.at[lo], RBR.at[hi])[i]
        return rcopy(src, dst, rs_s.at[i], rs_r.at[i], right if i < 3 else left)

    def input_parts(part, first, second, third):
        part(far_m)
        part_send(0).start()
        part_send(3).start()
        first()
        part(right_m)
        part_send(1).start()
        part(left_m)
        part_send(4).start()
        second()
        part(m)
        third()

    def input_forward():
        part_send(0).wait_recv()
        PS[right_m, lo] = (PS[right_m, lo].astype(F32) + RAL[...].astype(F32)).astype(BF)
        part_send(2).start()
        part_send(3).wait_recv()
        PS[left_m, hi] = (PS[left_m, hi].astype(F32) + RAR[...].astype(F32)).astype(BF)
        part_send(5).start()

    def input_total():
        for i in (1, 2, 4, 5):
            part_send(i).wait_recv()
        return PS[m].astype(F32) + RBL[...].astype(F32) + RBR[...].astype(F32)

    def qg_send(p, hh):
        return rcopy(
            QG.at[p, hh], QGX.at[p, ds(x, BLK), pl.ds(hh * HALF, HALF)],
            qg_s.at[p, hh], qg_r.at[p, hh], partner,
        )

    @pl.when(is_video)
    def _():
        def attend(p):
            blocks = [pl.ds(t * BLK, BLK) for t in range(4)]

            def scores(hh):
                cols = ds(2 * p + hh, HALF)
                head = pl.ds(hh * HALF, HALF)
                q = Q[p, :, head]
                u = U[p, :, head]
                q_t = q.T
                top = None
                for t in range(4):
                    s = nn(K[blocks[t], cols], q_t) + BIAS[...]
                    S[4 * hh + t] = s
                    high = jnp.max(s, axis=0, keepdims=True)
                    top = high if top is None else jnp.maximum(top, high)
                return cols, head, q, u, top

            def weights(hh, cols, u, top):
                u_t = u.T
                total = jnp.zeros_like(top)
                weighted = jnp.zeros_like(top)
                for t in range(4):
                    e = jnp.exp2((S[4 * hh + t] - top) * (FACTOR * LOG2_E))
                    d = nn(V[blocks[t], cols], u_t)
                    S[4 * hh + t] = e
                    DP[4 * hh + t] = d
                    total += jnp.sum(e, axis=0, keepdims=True)
                    weighted += jnp.sum(e * d, axis=0, keepdims=True)
                inverse = 1.0 / total
                return inverse, weighted * inverse

            def grads(hh, cols, head, q, u, inverse, mean):
                query_grad = None
                for t in range(4):
                    a = S[4 * hh + t] * inverse
                    GR[1, blocks[t], cols] = nn(a.astype(BF), u).astype(BF)
                    sg = (a * (DP[4 * hh + t] - mean) * FACTOR).astype(BF)
                    GR[0, blocks[t], cols] = nn(sg, q).astype(BF)
                    more = nn(KT[cols, blocks[t]], sg)
                    query_grad = more if query_grad is None else query_grad + more
                QG[p, hh] = query_grad.T.astype(BF)
                qg_send(p, hh).start()

            cols0, head0, q0, u0, top0 = scores(0)
            inverse0, mean0 = weights(0, cols0, u0, top0)
            cols1, head1, q1, u1, top1 = scores(1)
            grads(0, cols0, head0, q0, u0, inverse0, mean0)
            inverse1, mean1 = weights(1, cols1, u1, top1)
            grads(1, cols1, head1, q1, u1, inverse1, mean1)

        far = 1 - keep_kind

        def fold(p, i):
            return KEEP[p, i] + CR[p, i].astype(F32)

        def far_kind(yd):
            return (1 - keep_kind) * 2 + yd

        def near_kind(yd):
            return keep_kind * 2 + yd

        def x1_early(p):
            core_send(p, far).wait_recv()
            for i, yd in ((0, 1 - yl), (1, yl)):
                X1S[p, i] = fold(p, far_kind(yd)).astype(BF)
                x1_send(p, i).start()

        def x2_early(p, i):
            if i == 0:
                core_send(p, keep_kind).wait_recv()
            yd = (1 - yl, yl)[i]
            x1_send(p, i).wait_recv()
            total = fold(p, near_kind(yd)) + X1R[p, i].astype(F32)
            KEEP[p, near_kind(yd)] = total
            X2S[p, i] = total.astype(BF)

            @pl.when(x >= 2)
            def _():
                x2_send(p, i).start()

        def y_early(p):
            @pl.when(x < 2)
            def _():
                x2_send(p, 0).wait_recv()
                YS[p] = (KEEP[p, near_kind(1 - yl)] + X2R[p, 0].astype(F32)).astype(BF)
                y_send(p).start()

        def z_send(p, kind):
            return rcopy(
                ZS.at[p - 2, kind], ZR.at[p - 2, kind], z_s.at[p - 2, kind], z_r.at[p - 2, kind], yside
            )

        def y_late(p, kind):
            core_send(p, kind).wait_recv()
            ZS[p - 2, kind] = fold(p, 2 * kind + 1 - yl).astype(BF)
            z_send(p, kind).start()
            KEEP[p, 2 * kind + yl] = fold(p, 2 * kind + yl)

        def x1_late(p):
            z_send(p, far).wait_recv()
            X1S[p, 0] = (KEEP[p, far_kind(yl)] + ZR[p - 2, far].astype(F32)).astype(BF)
            x1_send(p, 0).start()

        def x2_late(p):
            z_send(p, keep_kind).wait_recv()
            x1_send(p, 0).wait_recv()
            total = KEEP[p, near_kind(yl)] + ZR[p - 2, keep_kind].astype(F32) + X1R[p, 0].astype(F32)
            KEEP[p, near_kind(yl)] = total
            X2S[p, 0] = total.astype(BF)

            @pl.when(x >= 2)
            def _():
                x2_send(p, 0).start()

        def pair(p):
            for half in range(2):
                q_send(p, half).wait_recv()
            attend(p)

        def weigh(p):
            for kind in (far, keep_kind):
                weight_part(p, kind, GR[kind, :, ds(p, BLK)])

        def step(p, carry):
            pair(p)

            @pl.when(p == 0)
            def _():
                weigh(0)

            @pl.when(p == 1)
            def _():
                x1_early(0)

            return carry

        lax.fori_loop(0, 4, step, 0)

        def part(d):
            rows = ds(d, BLK)
            for j in range(4):
                out = pl.ds(j * BLK, BLK)
                PS[d, :, out] = (nt(GR[0, rows], W[0, out]) + nt(GR[1, rows], W[1, out])).astype(BF)

        def first():
            x2_early(0, 0)
            weigh(1)
            x1_early(1)
            x2_early(0, 1)
            weigh(2)
            y_late(2, far)
            weigh(3)
            y_late(3, far)
            y_late(2, keep_kind)

        def second():
            x2_early(1, 0)
            y_late(3, keep_kind)

        input_parts(part, first, second, lambda: y_early(0))
        input_forward()
        x1_late(2)
        x2_early(1, 1)
        x1_late(3)
        y_early(1)
        x2_late(2)
        x2_late(3)
        ig[0] = input_total().astype(BF)

        @pl.when(x < 2)
        def _():
            for p in range(2):
                x2_send(p, 1).wait_recv()
                y_send(p).wait_recv()
                wg[0, :, pl.ds(p * BLK, BLK)] = (
                    KEEP[p, near_kind(yl)] + X2R[p, 1].astype(F32) + YR[p].astype(F32)
                )
            for p in range(2, 4):
                x2_send(p, 0).wait_recv()
                wg[0, :, pl.ds(p * BLK, BLK)] = KEEP[p, near_kind(yl)] + X2R[p, 0].astype(F32)

        @pl.when(x >= 2)
        def _():
            wg[...] = jnp.zeros_like(wg)

        for p in range(4):
            n = 2 if p < 2 else 1
            for i in range(2):
                qg_send(p, i).wait_send()
                core_send(p, i).wait_send()
            for i in range(n):
                x1_send(p, i).wait_send()
            if p >= 2:
                z_send(p, 0).wait_send()
                z_send(p, 1).wait_send()

        @pl.when(x >= 2)
        def _():
            for p in range(4):
                for i in range(2 if p < 2 else 1):
                    x2_send(p, i).wait_send()

        @pl.when(x < 2)
        def _():
            for p in range(2):
                y_send(p).wait_send()

    @pl.when(is_neural)
    def _():
        tiny = eighth // 2

        def spread(half, d, i, rows):
            s = TOKX.at[(x + 4 - d) % 4, rows]
            device = right if i % 2 == 0 else left
            return rcopy(s, s, ar_s.at[half, d - 1, i], ar_r.at[half, d - 1, i], device)

        def eighth_of(half, b):
            return ds(4 * half + b, eighth)

        def first_of(half, b):
            return ds(8 * half + 2 * b, tiny)

        def second_of(half, b):
            return ds(8 * half + 2 * b + 1, tiny)

        def spread_start(half):
            for d in (1, 3, 2):
                swap_recv(half, d).wait_recv()
                spread(half, d, 0, eighth_of(half, m)).start()
                spread(half, d, 1, eighth_of(half, m)).start()

        def spread_on(half):
            for d in (1, 3, 2):
                spread(half, d, 0, eighth_of(half, left_m)).wait_recv()
                spread(half, d, 2, first_of(half, left_m)).start()
                spread(half, d, 1, eighth_of(half, right_m)).wait_recv()
                spread(half, d, 3, second_of(half, right_m)).start()

        def spread_end():
            for d in (1, 3, 2):
                for half in range(2):
                    spread(half, d, 2, first_of(half, far_m)).wait_recv()
                    spread(half, d, 3, second_of(half, far_m)).wait_recv()
                FT[:, ds((x + 4 - d) % 4, BLK)] = TOKX[(x + 4 - d) % 4].T

        right_x, left_x, far_x = (x + 1) % 4, (x + 3) % 4, (x + 2) % 4

        def gather(p, i, block):
            rows = ds(block, BLK) if i < 4 else ds(2 * block + i - 4, HALF)
            cols = pl.ds((i // 2) * HALF, HALF) if i < 4 else pl.ds(0, BLK)
            s = QGX.at[p, rows, cols]
            return rcopy(s, s, xg_s.at[p, i], xg_r.at[p, i], xdev(right_x if i % 2 == 0 else left_x))

        def relay(p):
            for hh in range(2):
                qg_send(p, hh).wait_recv()
                gather(p, 2 * hh, x).start()
                gather(p, 2 * hh + 1, x).start()

        def relay_on(p):
            gather(p, 0, left_x).wait_recv()
            gather(p, 2, left_x).wait_recv()
            gather(p, 4, left_x).start()
            gather(p, 1, right_x).wait_recv()
            gather(p, 3, right_x).wait_recv()
            gather(p, 5, right_x).start()

        def chunk(p):
            gather(p, 4, far_x).wait_recv()
            gather(p, 5, far_x).wait_recv()
            weight_part(p, 0, QGX[p])

        def stage_y(p):
            core_send(p, 0).wait_recv()
            YS[p] = (KEEP[p, 1 - yl] + CR[p, 1 - yl].astype(F32)).astype(BF)
            y_send(p).start()
            KEEP[p, yl] = KEEP[p, yl] + CR[p, yl].astype(F32)

        def part(d):
            for j in range(4):
                out = pl.ds(j * BLK, BLK)
                total = None
                for p in range(4):
                    more = nt(QGX[p, ds(x, BLK)], W[d, out, pl.ds(p * BLK, BLK)])
                    total = more if total is None else total + more
                PS[d, :, out] = total.astype(BF)

        for d in (1, 3, 2):
            swap_send(1, d).start()
        spread_start(0)
        FT[:, ds(x, BLK)] = TOK[x].T
        spread_start(1)
        spread_on(0)
        relay(0)
        relay(1)
        spread_on(1)
        relay_on(0)
        relay(2)
        relay(3)

        def third():
            spread_end()
            chunk(0)
            relay_on(2)
            stage_y(0)

        input_parts(part, lambda: relay_on(1), lambda: None, third)
        input_forward()
        chunk(1)
        relay_on(3)
        stage_y(1)
        chunk(2)
        chunk(3)
        stage_y(2)
        stage_y(3)
        load_cot.wait()
        ig[0] = (input_total() + COT[...].astype(F32)).astype(BF)
        for p in range(4):
            y_send(p).wait_recv()
            wg[0, :, pl.ds(p * BLK, BLK)] = KEEP[p, yl] + YR[p].astype(F32)
        for p in range(4):
            core_send(p, 0).wait_send()
            y_send(p).wait_send()
            for i in range(4):
                gather(p, i, x).wait_send()
            gather(p, 4, left_x).wait_send()
            gather(p, 5, right_x).wait_send()
            for half in range(2):
                q_send(p, half).wait_send()
        for half in range(2):
            for d in (1, 3, 2):
                swap_send(half, d).wait_send()
                spread(half, d, 0, eighth_of(half, m)).wait_send()
                spread(half, d, 1, eighth_of(half, m)).wait_send()
                spread(half, d, 2, first_of(half, left_m)).wait_send()
                spread(half, d, 3, second_of(half, right_m)).wait_send()

    for half in range(2):
        for i in range(4):
            ring(half, i, m).wait_send()
        ring(half, 4, left_m).wait_send()
        ring(half, 5, right_m).wait_send()
    for i in range(6):
        part_send(i).wait_send()


def local(tokens, proj, cotangent, counts, frames):
    vmem = pltpu.VMEM
    dma = pltpu.SemaphoreType.DMA
    scratch = [
        pltpu.SMEM((1,), jnp.int32),
        vmem((1, BLK), jnp.int32),
        vmem((4, BLK, WIDE), BF),
        vmem((4, WIDE, WIDE), BF),
        vmem((BLK, WIDE), BF),
        vmem((BLK, WIDE), F32),
        vmem((4, BLK, BLK), BF),
        vmem((4, BLK, BLK), BF),
        vmem((BLK, BLK), F32),
        vmem((WIDE, WIDE), BF),
        vmem((WIDE, WIDE), BF),
        vmem((WIDE, WIDE), BF),
        vmem((8, BLK, BLK), F32),
        vmem((8, BLK, BLK), F32),
        vmem((2, WIDE, WIDE), BF),
        vmem((4, 2, BLK, HALF), BF),
        vmem((WIDE, WIDE), BF),
        vmem((4, BLK, WIDE), BF),
        vmem((4, WIDE, BLK), BF),
        vmem((4, 4, BLK, BLK), BF),
        vmem((4, 4, BLK, BLK), BF),
        vmem((4, 4, BLK, BLK), F32),
        vmem((4, 2, BLK, BLK), BF),
        vmem((4, 2, BLK, BLK), BF),
        vmem((4, 2, BLK, BLK), BF),
        vmem((4, 2, BLK, BLK), BF),
        vmem((4, BLK, BLK), BF),
        vmem((4, BLK, BLK), BF),
        vmem((2, 2, BLK, BLK), BF),
        vmem((2, 2, BLK, BLK), BF),
        vmem((4, BLK, WIDE), BF),
        vmem((HALF, WIDE), BF),
        vmem((HALF, WIDE), BF),
        vmem((BLK, WIDE), BF),
        vmem((BLK, WIDE), BF),
        dma((8,)),
        dma((2, 6)), dma((2, 6)),
        dma((4, 2)), dma((4, 2)),
        dma((4, 2)), dma((4, 2)),
        dma((2, 3)), dma((2, 3)),
        dma((2, 3, 4)), dma((2, 3, 4)),
        dma((4, 6)), dma((4, 6)),
        dma((4, 2)), dma((4, 2)),
        dma((4, 2)), dma((4, 2)),
        dma((4, 2)), dma((4, 2)),
        dma((4,)), dma((4,)),
        dma((2, 2)), dma((2, 2)),
        dma((6,)), dma((6,)),
    ]
    anywhere = pl.BlockSpec(memory_space=pl.ANY)
    in_vmem = pl.BlockSpec(memory_space=vmem)
    return pl.pallas_call(
        kernel,
        out_shape=(vmem((1, BLK, WIDE), BF), vmem((1, BLK, WIDE), F32)),
        in_specs=[
            anywhere, anywhere, anywhere, anywhere, anywhere,
        ],
        out_specs=(in_vmem, in_vmem),
        scratch_shapes=scratch,
        compiler_params=pltpu.CompilerParams(
            collective_id=0, has_side_effects=True, vmem_limit_bytes=56 * 2**20
        ),
        cost_estimate=pl.CostEstimate(
            flops=20 * 10**9, bytes_accessed=16 * 2**20, transcendentals=2**21
        ),
    )(tokens, proj, cotangent, counts, frames.reshape(1, BLK))


def solution(mesh):
    return jax.shard_map(
        local,
        mesh=mesh,
        in_specs=(
            P("group", "win", "mp"),
            P("group", None, "mp"),
            P("win", "mp"),
            P("win"),
            P("win"),
        ),
        out_specs=(P("group", "win", "mp"), P("group", "win", "mp")),
        check_vma=False,
    )
```

```python
import jax
import jax.numpy as jnp
from jax import lax
from jax.experimental import pallas as pl
from jax.experimental.pallas import tpu as pltpu
from jax.sharding import PartitionSpec as P

MESH = pl.DeviceIdType.MESH
BF = jnp.bfloat16
F32 = jnp.float32
FACTOR = 128 ** (-0.5)
LOG2_E = 1.4426950408889634
BLK = 256
WIDE = 1024
HALF = 128
PIECE = 64


def nn(a, b):
    return jnp.dot(a, b, preferred_element_type=F32)


def nt(a, b):
    return lax.dot_general(a, b, (((1,), (1,)), ((), ())), preferred_element_type=F32)


def tn(a, b):
    return lax.dot_general(a, b, (((0,), (0,)), ((), ())), preferred_element_type=F32)


def ds(i, size):
    return pl.ds(pl.multiple_of(i * size, size), size)


def rcopy(src, dst, send_sem, recv_sem, device):
    return pltpu.make_async_remote_copy(
        src_ref=src,
        dst_ref=dst,
        send_sem=send_sem,
        recv_sem=recv_sem,
        device_id=device,
        device_id_type=MESH,
    )


def kernel(
    tok, proj, cot, counts_hbm, frames_hbm, ig, wg,
    counts, frames, TOK, W, COT, ACC, Q, U, BIAS, K, KT, V, S, DP, GR, QG, FT, TOKX, QGX, PSUM,
    CS, CR, KEEP, X1S, X1R, X2S, X2R, YS, YR, ZS, ZR, PS, RAL, RAR, RBL, RBR,
    l_sem, ag_s, ag_r, q_s, q_r, qg_s, qg_r, aa_s, aa_r, ar_s, ar_r, xg_s, xg_r,
    cs_s, cs_r, x1_s, x1_r, x2_s, x2_r, y_s, y_r, z_s, z_r, rs_s, rs_r,
):
    g = lax.axis_index("group")
    w = lax.axis_index("win")
    m = lax.axis_index("mp")
    x = w // 4
    yl = (w // 2) % 2
    c = w % 2
    is_video = g == 0
    is_neural = g == 1
    right_m, left_m, far_m = (m + 1) % 4, (m + 3) % 4, (m + 2) % 4
    right, left = {"mp": right_m}, {"mp": left_m}
    partner = {"group": 1 - g}
    core = {"win": w + 1 - 2 * c}
    yside = {"win": w + 2 - 4 * yl}

    def xdev(xp):
        return {"win": xp * 4 + w % 4}

    xnear = xdev(x + 1 - 2 * (x % 2))
    xback = xdev(3 - x)
    keep_kind = ((x + 1) // 2) % 2

    load_tok = pltpu.make_async_copy(tok.at[0], TOK.at[m], l_sem.at[0])
    load_tok.start()
    load_cot = pltpu.make_async_copy(cot, COT, l_sem.at[1])

    def load_w(i, b):
        return pltpu.make_async_copy(proj.at[0, ds(b, WIDE)], W.at[b], l_sem.at[2 + i])

    order = (m, left_m, right_m, far_m)

    @pl.when(is_neural)
    def _():
        for i in range(4):
            load_w(i, order[i]).start()

    @pl.when(is_video)
    def _():
        for i in range(2):
            load_w(i, i).start()

    load_cot.start()
    load_counts = pltpu.make_async_copy(counts_hbm, counts, l_sem.at[6])
    load_frames = pltpu.make_async_copy(frames_hbm, frames, l_sem.at[7])
    load_counts.start()
    load_frames.start()

    barrier = pltpu.get_barrier_semaphore()
    greet = [right, left, partner, core, yside] + [xdev((x + d) % 4) for d in (1, 2, 3)]
    for device in greet:
        pl.semaphore_signal(barrier, inc=1, device_id=device, device_id_type=MESH)
    pl.semaphore_wait(barrier, len(greet))

    lo, hi = pl.ds(0, HALF), pl.ds(HALF, HALF)

    def ring(half, i, block):
        device = right if i in (0, 1, 4) else left
        start = half * HALF + (0 if i in (0, 3, 4) else PIECE)
        rows = pl.ds(start, PIECE)
        return rcopy(TOK.at[block, rows], TOK.at[block, rows], ag_s.at[half, i], ag_r.at[half, i], device)

    def ring_start(half):
        for i in (0, 2, 1, 3):
            ring(half, i, m).start()

    def ring_forward(half):
        ring(half, 0, left_m).wait_recv()
        ring(half, 4, left_m).start()
        ring(half, 2, right_m).wait_recv()
        ring(half, 5, right_m).start()

    def q_send(j, half):
        s = Q.at[j, pl.ds(half * HALF, HALF)]
        return rcopy(s, s, q_s.at[j, half], q_r.at[j, half], partner)

    def project(b, i, half):
        rows = pl.ds(half * HALF, HALF)

        @pl.when(is_video)
        def _():
            if i == 0 and half == 0:
                load_w(0, 0).wait()
                load_w(1, 1).wait()
            keys = ds(2 * b + half, HALF)
            for j in range(4):
                cols = pl.ds(j * BLK, BLK)
                K[keys, cols] = nn(TOK[b, rows], W[0, :, cols]).astype(BF)
                V[keys, cols] = nn(TOK[b, rows], W[1, :, cols]).astype(BF)
            FT[:, keys] = TOK[b, rows].T
            KT[:, keys] = K[keys].T

        @pl.when(is_neural)
        def _():
            if half == 0:
                load_w(i, b).wait()
            for j in range(4):
                cols = pl.ds(j * BLK, BLK)
                part = nn(TOK[b, rows], W[b, :, cols])
                if i == 0:
                    ACC[rows, cols] = part
                elif i < 3:
                    ACC[rows, cols] += part
                else:
                    Q[j, rows] = (ACC[rows, cols] + part).astype(BF)
                    q_send(j, half).start()

    eighth = HALF // 4

    def swap_send(half, d):
        rows = ds(4 * half + m, eighth)
        return rcopy(
            TOK.at[(x + d) % 4, rows], TOKX.at[x, rows],
            aa_s.at[half, d - 1], aa_r.at[half, d - 1], xdev((x + d) % 4),
        )

    def swap_recv(half, d):
        s = TOKX.at[(x + 4 - d) % 4, ds(4 * half + m, eighth)]
        return rcopy(s, s, aa_s.at[half, d - 1], aa_r.at[half, d - 1], xdev((x + d) % 4))

    load_tok.wait()
    ring_start(0)
    project(m, 0, 0)
    ring_forward(0)
    ring_start(1)
    ring(0, 1, left_m).wait_recv()
    project(left_m, 1, 0)
    ring(0, 3, right_m).wait_recv()
    project(right_m, 2, 0)
    ring(0, 4, far_m).wait_recv()
    ring(0, 5, far_m).wait_recv()
    project(far_m, 3, 0)

    @pl.when(is_neural)
    def _():
        for d in (1, 3, 2):
            swap_send(0, d).start()

    project(m, 0, 1)
    ring_forward(1)
    ring(1, 1, left_m).wait_recv()
    project(left_m, 1, 1)
    ring(1, 3, right_m).wait_recv()
    project(right_m, 2, 1)

    load_counts.wait()
    load_frames.wait()

    @pl.when(is_video)
    def _():
        load_cot.wait()
        live = lax.broadcasted_iota(jnp.int32, (BLK, BLK), 0) < counts[0]
        for j in range(4):
            part = COT[:, pl.ds(j * BLK, BLK)].astype(F32)
            U[j] = jnp.where(live, part, jnp.zeros_like(part)).astype(BF)
        key_frame = lax.broadcasted_iota(jnp.int32, (BLK, BLK), 0) >> 6
        BIAS[...] = jnp.where(key_frame <= frames[...], 0.0, -1e30).astype(F32)

    ring(1, 4, far_m).wait_recv()
    ring(1, 5, far_m).wait_recv()
    project(far_m, 3, 1)

    def core_send(p, kind):
        both = pl.ds(2 * kind, 2)
        return rcopy(CS.at[p, both], CR.at[p, both], cs_s.at[p, kind], cs_r.at[p, kind], core)

    def weight_part(p, kind, rhs):
        for yd in range(2):
            CS[p, kind * 2 + yd] = nn(FT[ds(2 * yd + 1 - c, BLK)], rhs).astype(BF)
        core_send(p, kind).start()
        for yd in range(2):
            KEEP[p, kind * 2 + yd] = nn(FT[ds(2 * yd + c, BLK)], rhs)

    def y_send(p):
        return rcopy(YS.at[p], YR.at[p], y_s.at[p], y_r.at[p], yside)

    def x1_send(p, i):
        return rcopy(X1S.at[p, i], X1R.at[p, i], x1_s.at[p, i], x1_r.at[p, i], xnear)

    def x2_send(p, i):
        return rcopy(X2S.at[p, i], X2R.at[p, i], x2_s.at[p, i], x2_r.at[p, i], xback)

    def part_send(i):
        src = (
            PS.at[far_m, lo], PS.at[right_m, hi], PS.at[right_m, lo],
            PS.at[far_m, hi], PS.at[left_m, lo], PS.at[left_m, hi],
        )[i]
        dst = (RAL, RBL.at[hi], RBL.at[lo], RAR, RBR.at[lo], RBR.at[hi])[i]
        return rcopy(src, dst, rs_s.at[i], rs_r.at[i], right if i < 3 else left)

    def input_parts(part, first, second, third):
        part(far_m)
        part_send(0).start()
        part_send(3).start()
        first()
        part(right_m)
        part_send(1).start()
        part(left_m)
        part_send(4).start()
        second()
        part(m)
        third()

    def input_forward():
        part_send(0).wait_recv()
        PS[right_m, lo] = (PS[right_m, lo].astype(F32) + RAL[...].astype(F32)).astype(BF)
        part_send(2).start()
        part_send(3).wait_recv()
        PS[left_m, hi] = (PS[left_m, hi].astype(F32) + RAR[...].astype(F32)).astype(BF)
        part_send(5).start()

    def input_total():
        for i in (1, 2, 4, 5):
            part_send(i).wait_recv()
        return PS[m].astype(F32) + RBL[...].astype(F32) + RBR[...].astype(F32)

    def qg_send(p, hh):
        return rcopy(
            QG.at[p, hh], QGX.at[p, ds(x, BLK), pl.ds(hh * HALF, HALF)],
            qg_s.at[p, hh], qg_r.at[p, hh], partner,
        )

    @pl.when(is_video)
    def _():
        def attend(p):
            blocks = [pl.ds(t * BLK, BLK) for t in range(4)]

            def scores(hh):
                cols = ds(2 * p + hh, HALF)
                head = pl.ds(hh * HALF, HALF)
                q = Q[p, :, head]
                u = U[p, :, head]
                q_t = q.T
                top = None
                for t in range(4):
                    s = nn(K[blocks[t], cols], q_t) + BIAS[...]
                    S[4 * hh + t] = s
                    high = jnp.max(s, axis=0, keepdims=True)
                    top = high if top is None else jnp.maximum(top, high)
                return cols, head, q, u, top

            def weights(hh, cols, u, top):
                u_t = u.T
                total = jnp.zeros_like(top)
                weighted = jnp.zeros_like(top)
                for t in range(4):
                    e = jnp.exp2((S[4 * hh + t] - top) * (FACTOR * LOG2_E))
                    d = nn(V[blocks[t], cols], u_t)
                    S[4 * hh + t] = e
                    DP[4 * hh + t] = d
                    total += jnp.sum(e, axis=0, keepdims=True)
                    weighted += jnp.sum(e * d, axis=0, keepdims=True)
                inverse = 1.0 / total
                return inverse, weighted * inverse

            def grads(hh, cols, head, q, u, inverse, mean):
                query_grad = None
                for t in range(4):
                    a = S[4 * hh + t] * inverse
                    GR[1, blocks[t], cols] = nn(a.astype(BF), u).astype(BF)
                    sg = (a * (DP[4 * hh + t] - mean) * FACTOR).astype(BF)
                    GR[0, blocks[t], cols] = nn(sg, q).astype(BF)
                    more = nn(KT[cols, blocks[t]], sg)
                    query_grad = more if query_grad is None else query_grad + more
                QG[p, hh] = query_grad.T.astype(BF)
                qg_send(p, hh).start()

            cols0, head0, q0, u0, top0 = scores(0)
            inverse0, mean0 = weights(0, cols0, u0, top0)
            cols1, head1, q1, u1, top1 = scores(1)
            grads(0, cols0, head0, q0, u0, inverse0, mean0)
            inverse1, mean1 = weights(1, cols1, u1, top1)
            grads(1, cols1, head1, q1, u1, inverse1, mean1)

        far = 1 - keep_kind

        def fold(p, i):
            return KEEP[p, i] + CR[p, i].astype(F32)

        def far_kind(yd):
            return (1 - keep_kind) * 2 + yd

        def near_kind(yd):
            return keep_kind * 2 + yd

        def x1_early(p):
            core_send(p, far).wait_recv()
            for i, yd in ((0, 1 - yl), (1, yl)):
                X1S[p, i] = fold(p, far_kind(yd)).astype(BF)
                x1_send(p, i).start()

        def x2_early(p, i):
            if i == 0:
                core_send(p, keep_kind).wait_recv()
            yd = (1 - yl, yl)[i]
            x1_send(p, i).wait_recv()
            total = fold(p, near_kind(yd)) + X1R[p, i].astype(F32)
            KEEP[p, near_kind(yd)] = total
            X2S[p, i] = total.astype(BF)

            @pl.when(x >= 2)
            def _():
                x2_send(p, i).start()

        def y_early(p):
            @pl.when(x < 2)
            def _():
                x2_send(p, 0).wait_recv()
                YS[p] = (KEEP[p, near_kind(1 - yl)] + X2R[p, 0].astype(F32)).astype(BF)
                y_send(p).start()

        def z_send(p, kind):
            return rcopy(
                ZS.at[p - 2, kind], ZR.at[p - 2, kind], z_s.at[p - 2, kind], z_r.at[p - 2, kind], yside
            )

        def y_late(p, kind):
            core_send(p, kind).wait_recv()
            ZS[p - 2, kind] = fold(p, 2 * kind + 1 - yl).astype(BF)
            z_send(p, kind).start()
            KEEP[p, 2 * kind + yl] = fold(p, 2 * kind + yl)

        def x1_late(p):
            z_send(p, far).wait_recv()
            X1S[p, 0] = (KEEP[p, far_kind(yl)] + ZR[p - 2, far].astype(F32)).astype(BF)
            x1_send(p, 0).start()

        def x2_late(p):
            z_send(p, keep_kind).wait_recv()
            x1_send(p, 0).wait_recv()
            total = KEEP[p, near_kind(yl)] + ZR[p - 2, keep_kind].astype(F32) + X1R[p, 0].astype(F32)
            KEEP[p, near_kind(yl)] = total
            X2S[p, 0] = total.astype(BF)

            @pl.when(x >= 2)
            def _():
                x2_send(p, 0).start()

        def pair(p):
            for half in range(2):
                q_send(p, half).wait_recv()
            attend(p)

        def weigh(p):
            for kind in (far, keep_kind):
                weight_part(p, kind, GR[kind, :, ds(p, BLK)])

        def step(p, carry):
            pair(p)

            @pl.when(p == 0)
            def _():
                weigh(0)

            @pl.when(p == 1)
            def _():
                x1_early(0)

            return carry

        lax.fori_loop(0, 4, step, 0)

        def part(d):
            rows = ds(d, BLK)
            for j in range(4):
                out = pl.ds(j * BLK, BLK)
                PS[d, :, out] = (nt(GR[0, rows], W[0, out]) + nt(GR[1, rows], W[1, out])).astype(BF)

        def first():
            x2_early(0, 0)
            weigh(2)
            y_late(2, far)
            weigh(1)
            x1_early(1)
            x2_early(0, 1)
            weigh(3)
            y_late(3, far)
            y_late(2, keep_kind)

        def second():
            x2_early(1, 0)
            y_late(3, keep_kind)

        input_parts(part, first, second, lambda: y_early(0))
        input_forward()
        x1_late(2)
        x2_early(1, 1)
        x1_late(3)
        y_early(1)
        x2_late(2)
        x2_late(3)
        ig[0] = input_total().astype(BF)

        @pl.when(x < 2)
        def _():
            for p in range(2):
                x2_send(p, 1).wait_recv()
                y_send(p).wait_recv()
                wg[0, :, pl.ds(p * BLK, BLK)] = (
                    KEEP[p, near_kind(yl)] + X2R[p, 1].astype(F32) + YR[p].astype(F32)
                )
            for p in range(2, 4):
                x2_send(p, 0).wait_recv()
                wg[0, :, pl.ds(p * BLK, BLK)] = KEEP[p, near_kind(yl)] + X2R[p, 0].astype(F32)

        @pl.when(x >= 2)
        def _():
            wg[...] = jnp.zeros_like(wg)

        for p in range(4):
            n = 2 if p < 2 else 1
            for i in range(2):
                qg_send(p, i).wait_send()
                core_send(p, i).wait_send()
            for i in range(n):
                x1_send(p, i).wait_send()
            if p >= 2:
                z_send(p, 0).wait_send()
                z_send(p, 1).wait_send()

        @pl.when(x >= 2)
        def _():
            for p in range(4):
                for i in range(2 if p < 2 else 1):
                    x2_send(p, i).wait_send()

        @pl.when(x < 2)
        def _():
            for p in range(2):
                y_send(p).wait_send()

    @pl.when(is_neural)
    def _():
        tiny = eighth // 2

        def spread(half, d, i, rows):
            s = TOKX.at[(x + 4 - d) % 4, rows]
            device = right if i % 2 == 0 else left
            return rcopy(s, s, ar_s.at[half, d - 1, i], ar_r.at[half, d - 1, i], device)

        def eighth_of(half, b):
            return ds(4 * half + b, eighth)

        def first_of(half, b):
            return ds(8 * half + 2 * b, tiny)

        def second_of(half, b):
            return ds(8 * half + 2 * b + 1, tiny)

        def spread_start(half):
            for d in (1, 3, 2):
                swap_recv(half, d).wait_recv()
                spread(half, d, 0, eighth_of(half, m)).start()
                spread(half, d, 1, eighth_of(half, m)).start()

        def spread_on(half):
            for d in (1, 3, 2):
                spread(half, d, 0, eighth_of(half, left_m)).wait_recv()
                spread(half, d, 2, first_of(half, left_m)).start()
                spread(half, d, 1, eighth_of(half, right_m)).wait_recv()
                spread(half, d, 3, second_of(half, right_m)).start()

        def spread_end():
            for d in (1, 3, 2):
                for half in range(2):
                    spread(half, d, 2, first_of(half, far_m)).wait_recv()
                    spread(half, d, 3, second_of(half, far_m)).wait_recv()
                FT[:, ds((x + 4 - d) % 4, BLK)] = TOKX[(x + 4 - d) % 4].T

        right_x, left_x, far_x = (x + 1) % 4, (x + 3) % 4, (x + 2) % 4

        def gather(p, i, block):
            rows = ds(block, BLK) if i < 4 else ds(2 * block + i - 4, HALF)
            cols = pl.ds((i // 2) * HALF, HALF) if i < 4 else pl.ds(0, BLK)
            s = QGX.at[p, rows, cols]
            return rcopy(s, s, xg_s.at[p, i], xg_r.at[p, i], xdev(right_x if i % 2 == 0 else left_x))

        def relay(p):
            for hh in range(2):
                qg_send(p, hh).wait_recv()
                gather(p, 2 * hh, x).start()
                gather(p, 2 * hh + 1, x).start()

        def relay_on(p):
            gather(p, 0, left_x).wait_recv()
            gather(p, 2, left_x).wait_recv()
            gather(p, 4, left_x).start()
            gather(p, 1, right_x).wait_recv()
            gather(p, 3, right_x).wait_recv()
            gather(p, 5, right_x).start()

        def chunk(p):
            gather(p, 4, far_x).wait_recv()
            gather(p, 5, far_x).wait_recv()
            weight_part(p, 0, QGX[p])

        def stage_y(p):
            core_send(p, 0).wait_recv()
            YS[p] = (KEEP[p, 1 - yl] + CR[p, 1 - yl].astype(F32)).astype(BF)
            y_send(p).start()
            KEEP[p, yl] = KEEP[p, yl] + CR[p, yl].astype(F32)

        def some_part(d, j, pairs):
            total = None
            for p in pairs:
                more = nt(QGX[p, ds(x, BLK)], W[d, pl.ds(j * BLK, BLK), pl.ds(p * BLK, BLK)])
                total = more if total is None else total + more
            return total

        def begin_parts(d, carry):
            for j in range(4):
                PSUM[d, :, pl.ds(j * BLK, BLK)] = some_part(d, j, (0, 1))
            return carry

        def add_parts(d, carry):
            for j in range(4):
                PSUM[d, :, pl.ds(j * BLK, BLK)] += some_part(d, j, (2,))
            return carry

        def part(d):
            for j in range(4):
                out = pl.ds(j * BLK, BLK)
                PS[d, :, out] = (PSUM[d, :, out] + some_part(d, j, (3,))).astype(BF)

        for d in (1, 3, 2):
            swap_send(1, d).start()
        spread_start(0)
        FT[:, ds(x, BLK)] = TOK[x].T
        spread_start(1)
        spread_on(0)
        relay(0)
        relay(1)
        lax.fori_loop(0, 4, begin_parts, 0)
        spread_on(1)
        relay_on(0)
        relay(2)
        lax.fori_loop(0, 4, add_parts, 0)
        relay(3)

        def third():
            spread_end()
            chunk(0)
            relay_on(2)
            stage_y(0)

        input_parts(part, lambda: relay_on(1), lambda: None, third)
        input_forward()
        chunk(1)
        relay_on(3)
        stage_y(1)
        chunk(2)
        chunk(3)
        stage_y(2)
        stage_y(3)
        load_cot.wait()
        ig[0] = (input_total() + COT[...].astype(F32)).astype(BF)
        for p in range(4):
            y_send(p).wait_recv()
            wg[0, :, pl.ds(p * BLK, BLK)] = KEEP[p, yl] + YR[p].astype(F32)
        for p in range(4):
            core_send(p, 0).wait_send()
            y_send(p).wait_send()
            for i in range(4):
                gather(p, i, x).wait_send()
            gather(p, 4, left_x).wait_send()
            gather(p, 5, right_x).wait_send()
            for half in range(2):
                q_send(p, half).wait_send()
        for half in range(2):
            for d in (1, 3, 2):
                swap_send(half, d).wait_send()
                spread(half, d, 0, eighth_of(half, m)).wait_send()
                spread(half, d, 1, eighth_of(half, m)).wait_send()
                spread(half, d, 2, first_of(half, left_m)).wait_send()
                spread(half, d, 3, second_of(half, right_m)).wait_send()

    for half in range(2):
        for i in range(4):
            ring(half, i, m).wait_send()
        ring(half, 4, left_m).wait_send()
        ring(half, 5, right_m).wait_send()
    for i in range(6):
        part_send(i).wait_send()


def local(tokens, proj, cotangent, counts, frames):
    vmem = pltpu.VMEM
    dma = pltpu.SemaphoreType.DMA
    scratch = [
        pltpu.SMEM((1,), jnp.int32),
        vmem((1, BLK), jnp.int32),
        vmem((4, BLK, WIDE), BF),
        vmem((4, WIDE, WIDE), BF),
        vmem((BLK, WIDE), BF),
        vmem((BLK, WIDE), F32),
        vmem((4, BLK, BLK), BF),
        vmem((4, BLK, BLK), BF),
        vmem((BLK, BLK), F32),
        vmem((WIDE, WIDE), BF),
        vmem((WIDE, WIDE), BF),
        vmem((WIDE, WIDE), BF),
        vmem((8, BLK, BLK), F32),
        vmem((8, BLK, BLK), F32),
        vmem((2, WIDE, WIDE), BF),
        vmem((4, 2, BLK, HALF), BF),
        vmem((WIDE, WIDE), BF),
        vmem((4, BLK, WIDE), BF),
        vmem((4, WIDE, BLK), BF),
        vmem((4, BLK, WIDE), F32),
        vmem((4, 4, BLK, BLK), BF),
        vmem((4, 4, BLK, BLK), BF),
        vmem((4, 4, BLK, BLK), F32),
        vmem((4, 2, BLK, BLK), BF),
        vmem((4, 2, BLK, BLK), BF),
        vmem((4, 2, BLK, BLK), BF),
        vmem((4, 2, BLK, BLK), BF),
        vmem((4, BLK, BLK), BF),
        vmem((4, BLK, BLK), BF),
        vmem((2, 2, BLK, BLK), BF),
        vmem((2, 2, BLK, BLK), BF),
        vmem((4, BLK, WIDE), BF),
        vmem((HALF, WIDE), BF),
        vmem((HALF, WIDE), BF),
        vmem((BLK, WIDE), BF),
        vmem((BLK, WIDE), BF),
        dma((8,)),
        dma((2, 6)), dma((2, 6)),
        dma((4, 2)), dma((4, 2)),
        dma((4, 2)), dma((4, 2)),
        dma((2, 3)), dma((2, 3)),
        dma((2, 3, 4)), dma((2, 3, 4)),
        dma((4, 6)), dma((4, 6)),
        dma((4, 2)), dma((4, 2)),
        dma((4, 2)), dma((4, 2)),
        dma((4, 2)), dma((4, 2)),
        dma((4,)), dma((4,)),
        dma((2, 2)), dma((2, 2)),
        dma((6,)), dma((6,)),
    ]
    anywhere = pl.BlockSpec(memory_space=pl.ANY)
    in_vmem = pl.BlockSpec(memory_space=vmem)
    return pl.pallas_call(
        kernel,
        out_shape=(vmem((1, BLK, WIDE), BF), vmem((1, BLK, WIDE), F32)),
        in_specs=[
            anywhere, anywhere, anywhere, anywhere, anywhere,
        ],
        out_specs=(in_vmem, in_vmem),
        scratch_shapes=scratch,
        compiler_params=pltpu.CompilerParams(
            collective_id=0, has_side_effects=True, vmem_limit_bytes=56 * 2**20
        ),
        cost_estimate=pl.CostEstimate(
            flops=20 * 10**9, bytes_accessed=16 * 2**20, transcendentals=2**21
        ),
    )(tokens, proj, cotangent, counts, frames.reshape(1, BLK))


def solution(mesh):
    return jax.shard_map(
        local,
        mesh=mesh,
        in_specs=(
            P("group", "win", "mp"),
            P("group", None, "mp"),
            P("win", "mp"),
            P("win"),
            P("win"),
        ),
        out_specs=(P("group", "win", "mp"), P("group", "win", "mp")),
        check_vma=False,
    )
```

```python
import jax
import jax.numpy as jnp
from jax import lax
from jax.experimental import pallas as pl
from jax.experimental.pallas import tpu as pltpu
from jax.sharding import PartitionSpec as P

MESH = pl.DeviceIdType.MESH
BF = jnp.bfloat16
F32 = jnp.float32
FACTOR = 128 ** (-0.5)
LOG2_E = 1.4426950408889634
BLK = 256
WIDE = 1024
HALF = 128
PIECE = 64


def nn(a, b):
    return jnp.dot(a, b, preferred_element_type=F32)


def nt(a, b):
    return lax.dot_general(a, b, (((1,), (1,)), ((), ())), preferred_element_type=F32)


def tn(a, b):
    return lax.dot_general(a, b, (((0,), (0,)), ((), ())), preferred_element_type=F32)


def ds(i, size):
    return pl.ds(pl.multiple_of(i * size, size), size)


def rcopy(src, dst, send_sem, recv_sem, device):
    return pltpu.make_async_remote_copy(
        src_ref=src,
        dst_ref=dst,
        send_sem=send_sem,
        recv_sem=recv_sem,
        device_id=device,
        device_id_type=MESH,
    )


def kernel(
    tok, proj, cot, counts_hbm, frames_hbm, ig, wg,
    counts, frames, TOK, W, COT, ACC, Q, U, BIAS, K, KT, V, S, DP, GR, QG, FT, TOKX, QGX, PSUM,
    CS, CR, KEEP, X1S, X1R, X2S, X2R, YS, YR, ZS, ZR, PS, RAL, RAR, RBL, RBR,
    l_sem, ag_s, ag_r, q_s, q_r, qg_s, qg_r, aa_s, aa_r, ar_s, ar_r, xg_s, xg_r,
    cs_s, cs_r, x1_s, x1_r, x2_s, x2_r, y_s, y_r, z_s, z_r, rs_s, rs_r,
):
    g = lax.axis_index("group")
    w = lax.axis_index("win")
    m = lax.axis_index("mp")
    x = w // 4
    yl = (w // 2) % 2
    c = w % 2
    is_video = g == 0
    is_neural = g == 1
    right_m, left_m, far_m = (m + 1) % 4, (m + 3) % 4, (m + 2) % 4
    right, left = {"mp": right_m}, {"mp": left_m}
    partner = {"group": 1 - g}
    core = {"win": w + 1 - 2 * c}
    yside = {"win": w + 2 - 4 * yl}

    def xdev(xp):
        return {"win": xp * 4 + w % 4}

    xnear = xdev(x + 1 - 2 * (x % 2))
    xback = xdev(3 - x)
    keep_kind = ((x + 1) // 2) % 2

    load_tok = pltpu.make_async_copy(tok.at[0], TOK.at[m], l_sem.at[0])
    load_tok.start()
    load_cot = pltpu.make_async_copy(cot, COT, l_sem.at[1])

    def load_w(i, b):
        return pltpu.make_async_copy(proj.at[0, ds(b, WIDE)], W.at[b], l_sem.at[2 + i])

    order = (m, left_m, right_m, far_m)

    @pl.when(is_neural)
    def _():
        for i in range(4):
            load_w(i, order[i]).start()

    @pl.when(is_video)
    def _():
        for i in range(2):
            load_w(i, i).start()

    load_cot.start()
    load_counts = pltpu.make_async_copy(counts_hbm, counts, l_sem.at[6])
    load_frames = pltpu.make_async_copy(frames_hbm, frames, l_sem.at[7])
    load_counts.start()
    load_frames.start()

    barrier = pltpu.get_barrier_semaphore()
    greet = [right, left, partner, core, yside] + [xdev((x + d) % 4) for d in (1, 2, 3)]
    for device in greet:
        pl.semaphore_signal(barrier, inc=1, device_id=device, device_id_type=MESH)
    pl.semaphore_wait(barrier, len(greet))

    lo, hi = pl.ds(0, HALF), pl.ds(HALF, HALF)

    def ring(half, i, block):
        device = right if i in (0, 1, 4) else left
        start = half * HALF + (0 if i in (0, 3, 4) else PIECE)
        rows = pl.ds(start, PIECE)
        return rcopy(TOK.at[block, rows], TOK.at[block, rows], ag_s.at[half, i], ag_r.at[half, i], device)

    def ring_start(half):
        for i in (0, 2, 1, 3):
            ring(half, i, m).start()

    def ring_forward(half):
        ring(half, 0, left_m).wait_recv()
        ring(half, 4, left_m).start()
        ring(half, 2, right_m).wait_recv()
        ring(half, 5, right_m).start()

    def q_send(j, half):
        s = Q.at[j, pl.ds(half * HALF, HALF)]
        return rcopy(s, s, q_s.at[j, half], q_r.at[j, half], partner)

    def project(b, i, half):
        rows = pl.ds(half * HALF, HALF)

        @pl.when(is_video)
        def _():
            if i == 0 and half == 0:
                load_w(0, 0).wait()
                load_w(1, 1).wait()
            keys = ds(2 * b + half, HALF)
            for j in range(4):
                cols = pl.ds(j * BLK, BLK)
                K[keys, cols] = nn(TOK[b, rows], W[0, :, cols]).astype(BF)
                V[keys, cols] = nn(TOK[b, rows], W[1, :, cols]).astype(BF)
            FT[:, keys] = TOK[b, rows].T
            KT[:, keys] = K[keys].T

        @pl.when(is_neural)
        def _():
            if half == 0:
                load_w(i, b).wait()
            for j in range(4):
                cols = pl.ds(j * BLK, BLK)
                part = nn(TOK[b, rows], W[b, :, cols])
                if i == 0:
                    ACC[rows, cols] = part
                elif i < 3:
                    ACC[rows, cols] += part
                else:
                    Q[j, rows] = (ACC[rows, cols] + part).astype(BF)
                    q_send(j, half).start()

    eighth = HALF // 4

    def swap_send(half, d):
        rows = ds(4 * half + m, eighth)
        return rcopy(
            TOK.at[(x + d) % 4, rows], TOKX.at[x, rows],
            aa_s.at[half, d - 1], aa_r.at[half, d - 1], xdev((x + d) % 4),
        )

    def swap_recv(half, d):
        s = TOKX.at[(x + 4 - d) % 4, ds(4 * half + m, eighth)]
        return rcopy(s, s, aa_s.at[half, d - 1], aa_r.at[half, d - 1], xdev((x + d) % 4))

    load_tok.wait()
    ring_start(0)
    project(m, 0, 0)
    ring_forward(0)
    ring_start(1)
    ring(0, 1, left_m).wait_recv()
    project(left_m, 1, 0)
    ring(0, 3, right_m).wait_recv()
    project(right_m, 2, 0)
    ring(0, 4, far_m).wait_recv()
    ring(0, 5, far_m).wait_recv()
    project(far_m, 3, 0)

    @pl.when(is_neural)
    def _():
        for d in (1, 3, 2):
            swap_send(0, d).start()

    project(m, 0, 1)
    ring_forward(1)
    ring(1, 1, left_m).wait_recv()
    project(left_m, 1, 1)
    ring(1, 3, right_m).wait_recv()
    project(right_m, 2, 1)

    load_counts.wait()
    load_frames.wait()

    @pl.when(is_video)
    def _():
        load_cot.wait()
        live = lax.broadcasted_iota(jnp.int32, (BLK, BLK), 0) < counts[0]
        for j in range(4):
            part = COT[:, pl.ds(j * BLK, BLK)].astype(F32)
            U[j] = jnp.where(live, part, jnp.zeros_like(part)).astype(BF)
        key_frame = lax.broadcasted_iota(jnp.int32, (BLK, BLK), 0) >> 6
        BIAS[...] = jnp.where(key_frame <= frames[...], 0.0, -1e30).astype(F32)

    ring(1, 4, far_m).wait_recv()
    ring(1, 5, far_m).wait_recv()
    project(far_m, 3, 1)

    def core_send(p, kind):
        both = pl.ds(2 * kind, 2)
        return rcopy(CS.at[p, both], CR.at[p, both], cs_s.at[p, kind], cs_r.at[p, kind], core)

    def weight_part(p, kind, rhs):
        for yd in range(2):
            CS[p, kind * 2 + yd] = nn(FT[ds(2 * yd + 1 - c, BLK)], rhs).astype(BF)
        core_send(p, kind).start()
        for yd in range(2):
            KEEP[p, kind * 2 + yd] = nn(FT[ds(2 * yd + c, BLK)], rhs)

    def y_send(p):
        return rcopy(YS.at[p], YR.at[p], y_s.at[p], y_r.at[p], yside)

    def x1_send(p, i):
        return rcopy(X1S.at[p, i], X1R.at[p, i], x1_s.at[p, i], x1_r.at[p, i], xnear)

    def x2_send(p, i):
        return rcopy(X2S.at[p, i], X2R.at[p, i], x2_s.at[p, i], x2_r.at[p, i], xback)

    def part_send(i):
        src = (
            PS.at[far_m, lo], PS.at[right_m, hi], PS.at[right_m, lo],
            PS.at[far_m, hi], PS.at[left_m, lo], PS.at[left_m, hi],
        )[i]
        dst = (RAL, RBL.at[hi], RBL.at[lo], RAR, RBR.at[lo], RBR.at[hi])[i]
        return rcopy(src, dst, rs_s.at[i], rs_r.at[i], right if i < 3 else left)

    def input_parts(part, first, second, third):
        part(far_m)
        part_send(0).start()
        part_send(3).start()
        first()
        part(right_m)
        part_send(1).start()
        part(left_m)
        part_send(4).start()
        second()
        part(m)
        third()

    def input_forward():
        part_send(0).wait_recv()
        PS[right_m, lo] = (PS[right_m, lo].astype(F32) + RAL[...].astype(F32)).astype(BF)
        part_send(2).start()
        part_send(3).wait_recv()
        PS[left_m, hi] = (PS[left_m, hi].astype(F32) + RAR[...].astype(F32)).astype(BF)
        part_send(5).start()

    def input_total():
        for i in (1, 2, 4, 5):
            part_send(i).wait_recv()
        return PS[m].astype(F32) + RBL[...].astype(F32) + RBR[...].astype(F32)

    def qg_send(p, hh):
        return rcopy(
            QG.at[p, hh], QGX.at[p, ds(x, BLK), pl.ds(hh * HALF, HALF)],
            qg_s.at[p, hh], qg_r.at[p, hh], partner,
        )

    @pl.when(is_video)
    def _():
        def attend(p):
            blocks = [pl.ds(t * BLK, BLK) for t in range(4)]

            def scores(hh):
                cols = ds(2 * p + hh, HALF)
                head = pl.ds(hh * HALF, HALF)
                q = Q[p, :, head]
                u = U[p, :, head]
                q_t = q.T
                top = None
                for t in range(4):
                    s = nn(K[blocks[t], cols], q_t) + BIAS[...]
                    S[4 * hh + t] = s
                    high = jnp.max(s, axis=0, keepdims=True)
                    top = high if top is None else jnp.maximum(top, high)
                return cols, head, q, u, top

            def weights(hh, cols, u, top):
                u_t = u.T
                total = jnp.zeros_like(top)
                weighted = jnp.zeros_like(top)
                for t in range(4):
                    e = jnp.exp2((S[4 * hh + t] - top) * (FACTOR * LOG2_E))
                    d = nn(V[blocks[t], cols], u_t)
                    S[4 * hh + t] = e
                    DP[4 * hh + t] = d
                    total += jnp.sum(e, axis=0, keepdims=True)
                    weighted += jnp.sum(e * d, axis=0, keepdims=True)
                inverse = 1.0 / total
                return inverse, weighted * inverse

            def grads(hh, cols, head, q, u, inverse, mean):
                query_grad = None
                for t in range(4):
                    a = S[4 * hh + t] * inverse
                    GR[1, blocks[t], cols] = nn(a.astype(BF), u).astype(BF)
                    sg = (a * (DP[4 * hh + t] - mean) * FACTOR).astype(BF)
                    GR[0, blocks[t], cols] = nn(sg, q).astype(BF)
                    more = nn(KT[cols, blocks[t]], sg)
                    query_grad = more if query_grad is None else query_grad + more
                QG[p, hh] = query_grad.T.astype(BF)
                qg_send(p, hh).start()

            cols0, head0, q0, u0, top0 = scores(0)
            inverse0, mean0 = weights(0, cols0, u0, top0)
            cols1, head1, q1, u1, top1 = scores(1)
            grads(0, cols0, head0, q0, u0, inverse0, mean0)
            inverse1, mean1 = weights(1, cols1, u1, top1)
            grads(1, cols1, head1, q1, u1, inverse1, mean1)

        far = 1 - keep_kind

        def fold(p, i):
            return KEEP[p, i] + CR[p, i].astype(F32)

        def far_kind(yd):
            return (1 - keep_kind) * 2 + yd

        def near_kind(yd):
            return keep_kind * 2 + yd

        def x1_early(p):
            core_send(p, far).wait_recv()
            for i, yd in ((0, 1 - yl), (1, yl)):
                X1S[p, i] = fold(p, far_kind(yd)).astype(BF)
                x1_send(p, i).start()

        def x2_early(p, i):
            if i == 0:
                core_send(p, keep_kind).wait_recv()
            yd = (1 - yl, yl)[i]
            x1_send(p, i).wait_recv()
            total = fold(p, near_kind(yd)) + X1R[p, i].astype(F32)
            KEEP[p, near_kind(yd)] = total
            X2S[p, i] = total.astype(BF)

            @pl.when(x >= 2)
            def _():
                x2_send(p, i).start()

        def y_early(p):
            @pl.when(x < 2)
            def _():
                x2_send(p, 0).wait_recv()
                YS[p] = (KEEP[p, near_kind(1 - yl)] + X2R[p, 0].astype(F32)).astype(BF)
                y_send(p).start()

        def z_send(p, kind):
            return rcopy(
                ZS.at[p - 2, kind], ZR.at[p - 2, kind], z_s.at[p - 2, kind], z_r.at[p - 2, kind], yside
            )

        def y_late(p, kind):
            core_send(p, kind).wait_recv()
            ZS[p - 2, kind] = fold(p, 2 * kind + 1 - yl).astype(BF)
            z_send(p, kind).start()
            KEEP[p, 2 * kind + yl] = fold(p, 2 * kind + yl)

        def x1_late(p):
            z_send(p, far).wait_recv()
            X1S[p, 0] = (KEEP[p, far_kind(yl)] + ZR[p - 2, far].astype(F32)).astype(BF)
            x1_send(p, 0).start()

        def x2_late(p):
            z_send(p, keep_kind).wait_recv()
            x1_send(p, 0).wait_recv()
            total = KEEP[p, near_kind(yl)] + ZR[p - 2, keep_kind].astype(F32) + X1R[p, 0].astype(F32)
            KEEP[p, near_kind(yl)] = total
            X2S[p, 0] = total.astype(BF)

            @pl.when(x >= 2)
            def _():
                x2_send(p, 0).start()

        def pair(p):
            for half in range(2):
                q_send(p, half).wait_recv()
            attend(p)

        def weigh(p):
            for kind in (far, keep_kind):
                weight_part(p, kind, GR[kind, :, ds(p, BLK)])

        def step(p, carry):
            pair(p)

            @pl.when(p == 0)
            def _():
                weigh(0)

            @pl.when(p == 1)
            def _():
                x1_early(0)

            return carry

        lax.fori_loop(0, 4, step, 0)

        def part(d):
            rows = ds(d, BLK)
            for j in range(4):
                out = pl.ds(j * BLK, BLK)
                PS[d, :, out] = (nt(GR[0, rows], W[0, out]) + nt(GR[1, rows], W[1, out])).astype(BF)

        def first():
            x2_early(0, 0)
            weigh(2)
            y_late(2, far)
            weigh(1)
            x1_early(1)
            x2_early(0, 1)
            weigh(3)
            y_late(3, far)
            y_late(2, keep_kind)

        def second():
            y_late(3, keep_kind)
            x2_early(1, 0)

        input_parts(part, first, second, lambda: y_early(0))
        input_forward()
        x1_late(2)
        x2_early(1, 1)
        x1_late(3)
        y_early(1)
        x2_late(2)
        x2_late(3)
        ig[0] = input_total().astype(BF)

        @pl.when(x < 2)
        def _():
            for p in range(2):
                x2_send(p, 1).wait_recv()
                y_send(p).wait_recv()
                wg[0, :, pl.ds(p * BLK, BLK)] = (
                    KEEP[p, near_kind(yl)] + X2R[p, 1].astype(F32) + YR[p].astype(F32)
                )
            for p in range(2, 4):
                x2_send(p, 0).wait_recv()
                wg[0, :, pl.ds(p * BLK, BLK)] = KEEP[p, near_kind(yl)] + X2R[p, 0].astype(F32)

        @pl.when(x >= 2)
        def _():
            wg[...] = jnp.zeros_like(wg)

        for p in range(4):
            n = 2 if p < 2 else 1
            for i in range(2):
                qg_send(p, i).wait_send()
                core_send(p, i).wait_send()
            for i in range(n):
                x1_send(p, i).wait_send()
            if p >= 2:
                z_send(p, 0).wait_send()
                z_send(p, 1).wait_send()

        @pl.when(x >= 2)
        def _():
            for p in range(4):
                for i in range(2 if p < 2 else 1):
                    x2_send(p, i).wait_send()

        @pl.when(x < 2)
        def _():
            for p in range(2):
                y_send(p).wait_send()

    @pl.when(is_neural)
    def _():
        tiny = eighth // 2

        def spread(half, d, i, rows):
            s = TOKX.at[(x + 4 - d) % 4, rows]
            device = right if i % 2 == 0 else left
            return rcopy(s, s, ar_s.at[half, d - 1, i], ar_r.at[half, d - 1, i], device)

        def eighth_of(half, b):
            return ds(4 * half + b, eighth)

        def first_of(half, b):
            return ds(8 * half + 2 * b, tiny)

        def second_of(half, b):
            return ds(8 * half + 2 * b + 1, tiny)

        def spread_start(half):
            for d in (1, 3, 2):
                swap_recv(half, d).wait_recv()
                spread(half, d, 0, eighth_of(half, m)).start()
                spread(half, d, 1, eighth_of(half, m)).start()

        def spread_on(half):
            for d in (1, 3, 2):
                spread(half, d, 0, eighth_of(half, left_m)).wait_recv()
                spread(half, d, 2, first_of(half, left_m)).start()
                spread(half, d, 1, eighth_of(half, right_m)).wait_recv()
                spread(half, d, 3, second_of(half, right_m)).start()

        def spread_end():
            for d in (1, 3, 2):
                for half in range(2):
                    spread(half, d, 2, first_of(half, far_m)).wait_recv()
                    spread(half, d, 3, second_of(half, far_m)).wait_recv()
                FT[:, ds((x + 4 - d) % 4, BLK)] = TOKX[(x + 4 - d) % 4].T

        right_x, left_x, far_x = (x + 1) % 4, (x + 3) % 4, (x + 2) % 4

        def gather(p, i, block):
            rows = ds(block, BLK) if i < 4 else ds(2 * block + i - 4, HALF)
            cols = pl.ds((i // 2) * HALF, HALF) if i < 4 else pl.ds(0, BLK)
            s = QGX.at[p, rows, cols]
            return rcopy(s, s, xg_s.at[p, i], xg_r.at[p, i], xdev(right_x if i % 2 == 0 else left_x))

        def relay(p):
            for hh in range(2):
                qg_send(p, hh).wait_recv()
                gather(p, 2 * hh, x).start()
                gather(p, 2 * hh + 1, x).start()

        def relay_on(p):
            gather(p, 0, left_x).wait_recv()
            gather(p, 2, left_x).wait_recv()
            gather(p, 4, left_x).start()
            gather(p, 1, right_x).wait_recv()
            gather(p, 3, right_x).wait_recv()
            gather(p, 5, right_x).start()

        def chunk(p):
            gather(p, 4, far_x).wait_recv()
            gather(p, 5, far_x).wait_recv()
            weight_part(p, 0, QGX[p])

        def stage_y(p):
            core_send(p, 0).wait_recv()
            YS[p] = (KEEP[p, 1 - yl] + CR[p, 1 - yl].astype(F32)).astype(BF)
            y_send(p).start()
            KEEP[p, yl] = KEEP[p, yl] + CR[p, yl].astype(F32)

        def some_part(d, j, pairs):
            total = None
            for p in pairs:
                more = nt(QGX[p, ds(x, BLK)], W[d, pl.ds(j * BLK, BLK), pl.ds(p * BLK, BLK)])
                total = more if total is None else total + more
            return total

        def begin_parts(d, carry):
            for j in range(4):
                PSUM[d, :, pl.ds(j * BLK, BLK)] = some_part(d, j, (0, 1))
            return carry

        def add_parts(d, carry):
            for j in range(4):
                PSUM[d, :, pl.ds(j * BLK, BLK)] += some_part(d, j, (2,))
            return carry

        def part(d):
            for j in range(4):
                out = pl.ds(j * BLK, BLK)
                PS[d, :, out] = (PSUM[d, :, out] + some_part(d, j, (3,))).astype(BF)

        for d in (1, 3, 2):
            swap_send(1, d).start()
        spread_start(0)
        FT[:, ds(x, BLK)] = TOK[x].T
        spread_start(1)
        spread_on(0)
        relay(0)
        relay(1)
        lax.fori_loop(0, 4, begin_parts, 0)
        spread_on(1)
        relay_on(0)
        relay(2)
        lax.fori_loop(0, 4, add_parts, 0)
        relay(3)

        def third():
            spread_end()
            chunk(0)
            relay_on(2)
            stage_y(0)

        input_parts(part, lambda: relay_on(1), lambda: None, third)
        input_forward()
        chunk(1)
        relay_on(3)
        stage_y(1)
        chunk(2)
        chunk(3)
        stage_y(2)
        stage_y(3)
        load_cot.wait()
        ig[0] = (input_total() + COT[...].astype(F32)).astype(BF)
        for p in range(4):
            y_send(p).wait_recv()
            wg[0, :, pl.ds(p * BLK, BLK)] = KEEP[p, yl] + YR[p].astype(F32)
        for p in range(4):
            core_send(p, 0).wait_send()
            y_send(p).wait_send()
            for i in range(4):
                gather(p, i, x).wait_send()
            gather(p, 4, left_x).wait_send()
            gather(p, 5, right_x).wait_send()
            for half in range(2):
                q_send(p, half).wait_send()
        for half in range(2):
            for d in (1, 3, 2):
                swap_send(half, d).wait_send()
                spread(half, d, 0, eighth_of(half, m)).wait_send()
                spread(half, d, 1, eighth_of(half, m)).wait_send()
                spread(half, d, 2, first_of(half, left_m)).wait_send()
                spread(half, d, 3, second_of(half, right_m)).wait_send()

    for half in range(2):
        for i in range(4):
            ring(half, i, m).wait_send()
        ring(half, 4, left_m).wait_send()
        ring(half, 5, right_m).wait_send()
    for i in range(6):
        part_send(i).wait_send()


def local(tokens, proj, cotangent, counts, frames):
    vmem = pltpu.VMEM
    dma = pltpu.SemaphoreType.DMA
    scratch = [
        pltpu.SMEM((1,), jnp.int32),
        vmem((1, BLK), jnp.int32),
        vmem((4, BLK, WIDE), BF),
        vmem((4, WIDE, WIDE), BF),
        vmem((BLK, WIDE), BF),
        vmem((BLK, WIDE), F32),
        vmem((4, BLK, BLK), BF),
        vmem((4, BLK, BLK), BF),
        vmem((BLK, BLK), F32),
        vmem((WIDE, WIDE), BF),
        vmem((WIDE, WIDE), BF),
        vmem((WIDE, WIDE), BF),
        vmem((8, BLK, BLK), F32),
        vmem((8, BLK, BLK), F32),
        vmem((2, WIDE, WIDE), BF),
        vmem((4, 2, BLK, HALF), BF),
        vmem((WIDE, WIDE), BF),
        vmem((4, BLK, WIDE), BF),
        vmem((4, WIDE, BLK), BF),
        vmem((4, BLK, WIDE), F32),
        vmem((4, 4, BLK, BLK), BF),
        vmem((4, 4, BLK, BLK), BF),
        vmem((4, 4, BLK, BLK), F32),
        vmem((4, 2, BLK, BLK), BF),
        vmem((4, 2, BLK, BLK), BF),
        vmem((4, 2, BLK, BLK), BF),
        vmem((4, 2, BLK, BLK), BF),
        vmem((4, BLK, BLK), BF),
        vmem((4, BLK, BLK), BF),
        vmem((2, 2, BLK, BLK), BF),
        vmem((2, 2, BLK, BLK), BF),
        vmem((4, BLK, WIDE), BF),
        vmem((HALF, WIDE), BF),
        vmem((HALF, WIDE), BF),
        vmem((BLK, WIDE), BF),
        vmem((BLK, WIDE), BF),
        dma((8,)),
        dma((2, 6)), dma((2, 6)),
        dma((4, 2)), dma((4, 2)),
        dma((4, 2)), dma((4, 2)),
        dma((2, 3)), dma((2, 3)),
        dma((2, 3, 4)), dma((2, 3, 4)),
        dma((4, 6)), dma((4, 6)),
        dma((4, 2)), dma((4, 2)),
        dma((4, 2)), dma((4, 2)),
        dma((4, 2)), dma((4, 2)),
        dma((4,)), dma((4,)),
        dma((2, 2)), dma((2, 2)),
        dma((6,)), dma((6,)),
    ]
    anywhere = pl.BlockSpec(memory_space=pl.ANY)
    in_vmem = pl.BlockSpec(memory_space=vmem)
    return pl.pallas_call(
        kernel,
        out_shape=(vmem((1, BLK, WIDE), BF), vmem((1, BLK, WIDE), F32)),
        in_specs=[
            anywhere, anywhere, anywhere, anywhere, anywhere,
        ],
        out_specs=(in_vmem, in_vmem),
        scratch_shapes=scratch,
        compiler_params=pltpu.CompilerParams(
            collective_id=0, has_side_effects=True, vmem_limit_bytes=56 * 2**20
        ),
        cost_estimate=pl.CostEstimate(
            flops=20 * 10**9, bytes_accessed=16 * 2**20, transcendentals=2**21
        ),
    )(tokens, proj, cotangent, counts, frames.reshape(1, BLK))


def solution(mesh):
    return jax.shard_map(
        local,
        mesh=mesh,
        in_specs=(
            P("group", "win", "mp"),
            P("group", None, "mp"),
            P("win", "mp"),
            P("win"),
            P("win"),
        ),
        out_specs=(P("group", "win", "mp"), P("group", "win", "mp")),
        check_vma=False,
    )
```
